1024 devices in a mesh: row: 8 (over z_lo, core), col: 128 (over y, x, z_hi).
Axes of the slice: x: 8, y: 8, z: 8 (z_hi: 2, z_lo: 4; z = z_hi * 4 + z_lo), core: 2. Of those that a mesh axis runs over, the one named last changes fastest.
Arguments:
- basis_block: float32 [32, 131072], P(None, ('row', 'col')), may hold values from -40 to 40
- previous: float32 [32, 131072], P(None, ('row', 'col')), may hold values from -6 to 6
- coupling: float32 [32, 32], replicated, may hold values from -2 to 2, as said below
- energies: float32 [131072], P(('row', 'col')), may hold values from 0.5 to 5
- tile_values: float32 [8, 128, 16, 128, 128], P('row', 'col'), may hold values from -0.125 to 0.125
- tile_rows: int32 [8, 128, 16], P('row', 'col'), may hold values from 0 to 127, as said below
- tile_cols: int32 [8, 128, 16], P('row', 'col'), may hold values from 0 to 7
- counts: int32 [8, 128], P('row', 'col'), may hold values from 12 to 16, as said below
Outputs:
- alpha_block: float32 [32, 32], replicated
- beta_block: float32 [32, 32], replicated
- basis_next: float32 [32, 131072], P(None, ('row', 'col'))
The draws below stay inside these ranges and needn't reach their ends.
Inputs may be any that keep to these rules, and one draw needn't show every extreme that they name: `coupling`: upper triangular with a positive diagonal. Slots 0 to counts - 1 of a device hold its tiles, the others are unused; some device has all 16 slots live. `tile_rows`: the first min(16, 128) slots of a device name different tile rows; beyond those, slots of one device may name the same tile position and their tiles then add.
All inputs are finite; a program needn't handle non-finite values.
Results may differ from the reference program's by a relative error of at most 0.0003.
Values sent between devices are 32-bit elements; how exact they have to be, the bound alone decides.
A program may use at most 32 MiB of HBM per device.

```python
import math
import jax
import jax.numpy as jnp
from jax import lax

K = 32
TILE = 128
PIECE = 128
SLOTS = 16
NSTATE = 131072
ATILES = 128
BTILES = 8
N_ROW = 8
N_COL = 128


def draw_basis_block(key, part):
    key_scale, key_noise = jax.random.split(key, 2)
    noise = jnp.clip(jax.random.normal(key_noise, (K, NSTATE), jnp.float32), -6.0, 6.0)
    scales = jnp.exp(jax.random.uniform(key_scale, (NSTATE,), jnp.float32, 0.0, jnp.log(10.0)))
    unscaled = scales[None, :] * noise
    gram_block = jnp.dot(unscaled, unscaled.T, precision=lax.Precision.HIGHEST, preferred_element_type=jnp.float32) / NSTATE
    lower_factor = jnp.linalg.cholesky(gram_block)
    return jax.scipy.linalg.solve_triangular(lower_factor, unscaled, lower=True)


def draw_coupling(key, part):
    key_upper, key_diagonal = jax.random.split(jax.random.fold_in(key, 7), 2)
    entries = jnp.clip(jax.random.normal(key_upper, (K, K), jnp.float32), -6.0, 6.0)
    strict_upper = jnp.triu(0.3 * entries, 1)
    diagonal_part = jax.random.uniform(key_diagonal, (K,), jnp.float32, 0.5, 1.5)
    return strict_upper + jnp.diag(diagonal_part)


def draw_tile_rows(key, part):
    repeats = -(-SLOTS // ATILES)
    device_keys = jax.random.split(jax.random.fold_in(key, 13), N_ROW * N_COL)

    def one_device(device_key):
        order = jax.random.permutation(device_key, repeats * ATILES)
        return (order % ATILES)[:SLOTS]
    rows_all = jax.vmap(one_device)(device_keys)
    return rows_all.reshape(N_ROW, N_COL, SLOTS).astype(jnp.int32)


def draw_counts(key, part):
    key_first, key_chosen = jax.random.split(jax.random.fold_in(key, 11), 2)
    low_count = SLOTS * 3 // 4
    flat_counts = jax.random.randint(key_first, (N_ROW * N_COL,), low_count, SLOTS + 1)
    chosen = jax.random.randint(key_chosen, (), 0, N_ROW * N_COL)
    flat_counts = jnp.where(jnp.arange(N_ROW * N_COL) == chosen, SLOTS, flat_counts)
    return flat_counts.reshape(N_ROW, N_COL).astype(jnp.int32)


def with_ends(result, stream_key, least, high):
    longest = result.shape.index(max(result.shape))
    spots = []
    for shift in (0, 1):
        where = [jax.random.randint(jax.random.fold_in(stream_key, axis), (), 0, length) for axis, length in enumerate(result.shape)]
        where[longest] = (where[longest] + shift) % result.shape[longest]
        spots.append(tuple(where))
    return result.at[spots[0]].set(least).at[spots[1]].set(high)


def steps_of(stream_key, extent, cuts, least, largest):
    def one(axis_at, blocks):
        heights = jax.random.uniform(jax.random.fold_in(jax.random.fold_in(stream_key, 6), axis_at), (blocks,), jnp.float32, least / len(cuts), largest / len(cuts))
        return jnp.repeat(jnp.exp(heights), extent[axis_at] // blocks).reshape((-1,) + (1,) * (len(extent) - axis_at - 1))

    factor_of = one(*cuts[0])
    for cut in cuts[1:]:
        factor_of = factor_of * one(*cut)
    return factor_of


def bell_draw(key, dims, deviation, bound, shards=(), kind=jnp.bfloat16):
    array = deviation * jax.random.normal(key, dims, jnp.float32)
    if shards:
        array = array * steps_of(key, dims, shards, -0.22, 0.18)
    return jnp.clip(array, -bound, bound).astype(kind)


def setup_inputs(seed: int = 0) -> dict:
    keys = jax.random.split(jax.random.key(seed), 9)
    return {
        "basis_block": draw_basis_block(jax.random.fold_in(keys[8], 71), 0),
        "previous": bell_draw(keys[1], (K, NSTATE), 1.0, 6.0, ((1, 1024),), jnp.float32),
        "coupling": draw_coupling(jax.random.fold_in(keys[8], 71), 0),
        "energies": jnp.clip(jnp.exp(math.log(5.0) - 2.3025851 * jax.random.uniform(keys[3], (NSTATE,), jnp.float32) ** steps_of(keys[3], (NSTATE,), ((0, 1024),), -0.2, 0.2)), 0.5, 5.0),
        "tile_values": bell_draw(keys[4], (N_ROW, N_COL, SLOTS, TILE, TILE), (SLOTS * TILE * TILE // PIECE) ** -0.5, 0.125, ((0, 8), (1, 128)), jnp.float32),
        "tile_rows": draw_tile_rows(jax.random.fold_in(keys[8], 71), 0),
        "tile_cols": with_ends(jax.random.randint(keys[6], (N_ROW, N_COL, SLOTS), 0, BTILES), jax.random.fold_in(keys[6], 1), 0, BTILES - 1).astype(jnp.int32),
        "counts": draw_counts(jax.random.fold_in(keys[8], 71), 0),
    }


def reference(basis_block, previous, coupling, energies, tile_values, tile_rows, tile_cols, counts):
    highest = lax.Precision.HIGHEST
    piece_tiles = PIECE // TILE
    blocks = basis_block.reshape(K, N_ROW, N_COL, piece_tiles, TILE)
    device_count = N_ROW * N_COL
    tile_sets = tile_values.reshape(device_count, SLOTS, TILE, TILE)
    slot_rows = tile_rows.reshape(device_count, SLOTS)
    slot_cols = tile_cols.reshape(device_count, SLOTS)
    live_counts = counts.reshape(device_count)
    device_ids = jnp.arange(device_count, dtype=jnp.int32)

    def device_step(accumulated, device_items):
        tile_set, row_list, col_list, live_count, device_id = device_items
        row_id = (device_id // N_COL).astype(jnp.int32)
        col_id = (device_id % N_COL).astype(jnp.int32)
        row_states = lax.dynamic_index_in_dim(blocks, row_id, 1, keepdims=False)
        row_states = row_states.reshape(K, ATILES, TILE).transpose(1, 0, 2)
        col_states = lax.dynamic_index_in_dim(blocks, col_id, 2, keepdims=False)
        col_states = col_states.reshape(K, BTILES, TILE).transpose(1, 0, 2)
        live_mask = (jnp.arange(SLOTS) < live_count).astype(jnp.float32)
        picked_cols = jnp.take(col_states, col_list, axis=0)
        picked_rows = jnp.take(row_states, row_list, axis=0)
        direct = jnp.einsum('sij,skj->ski', tile_set.astype(jnp.float32), picked_cols.astype(jnp.float32), precision=highest, preferred_element_type=jnp.float32) * live_mask[:, None, None]
        mirror = jnp.einsum('sij,ski->skj', tile_set.astype(jnp.float32), picked_rows.astype(jnp.float32), precision=highest, preferred_element_type=jnp.float32) * live_mask[:, None, None]
        row_sums = jax.ops.segment_sum(direct, row_list, num_segments=ATILES)
        col_sums = jax.ops.segment_sum(mirror, col_list, num_segments=BTILES)
        row_sums = row_sums.transpose(1, 0, 2).reshape(K, 1, N_COL, piece_tiles, TILE)
        col_sums = col_sums.transpose(1, 0, 2).reshape(K, N_ROW, 1, piece_tiles, TILE)
        zero_index = jnp.zeros((), jnp.int32)
        row_start = (zero_index, row_id, zero_index, zero_index, zero_index)
        current = lax.dynamic_slice(accumulated, row_start, row_sums.shape)
        accumulated = lax.dynamic_update_slice(accumulated, current + row_sums, row_start)
        col_start = (zero_index, zero_index, col_id, zero_index, zero_index)
        current = lax.dynamic_slice(accumulated, col_start, col_sums.shape)
        accumulated = lax.dynamic_update_slice(accumulated, current + col_sums, col_start)
        return (accumulated, None)
    initial = jnp.zeros((K, N_ROW, N_COL, piece_tiles, TILE), jnp.float32)
    accumulated, _ = lax.scan(device_step, initial, (tile_sets, slot_rows, slot_cols, live_counts, device_ids))
    offdiag_part = accumulated.reshape(K, NSTATE)
    applied = energies[None, :] * basis_block + offdiag_part - jnp.dot(coupling.astype(jnp.float32), previous.astype(jnp.float32), precision=highest, preferred_element_type=jnp.float32)
    alpha_block = jnp.dot(basis_block.astype(jnp.float32), applied.T.astype(jnp.float32), precision=highest, preferred_element_type=jnp.float32) / NSTATE
    residual = applied - jnp.dot(alpha_block.T.astype(jnp.float32), basis_block.astype(jnp.float32), precision=highest, preferred_element_type=jnp.float32)
    gram_block = jnp.dot(residual.astype(jnp.float32), residual.T.astype(jnp.float32), precision=highest, preferred_element_type=jnp.float32) / NSTATE
    lower_factor = jnp.linalg.cholesky(gram_block)
    basis_next = jax.scipy.linalg.solve_triangular(lower_factor, residual, lower=True)
    return (alpha_block, lower_factor.T, basis_next)
```

```python
import functools

import jax
import jax.numpy as jnp
from jax import lax
from jax.experimental import pallas as pl
from jax.experimental.pallas import tpu as pltpu
from jax.sharding import Mesh
from jax.sharding import PartitionSpec as P

AXES = ("zl", "co", "y", "x", "zh")
ROW = ("zl", "co")
COL = ("y", "x", "zh")
K = 32
HALF = 16
LEN = 128
SLOTS = 16
RING = 8
MESH = pl.DeviceIdType.MESH
HIGHEST = lax.Precision.HIGHEST
NT = (((1,), (1,)), ((), ()))
NN = (((1,), (0,)), ((), ()))


def split(value):
    high = value.astype(jnp.bfloat16)
    low = (value - high.astype(jnp.float32)).astype(jnp.bfloat16)
    return high, low


def dot_three(left, right, dims):
    lh, ll = left
    rh, rl = right
    both = lax.dot_general(
        jnp.concatenate([lh, ll], axis=0), rh, dims, preferred_element_type=jnp.float32
    )
    rest = lax.dot_general(lh, rl, dims, preferred_element_type=jnp.float32)
    return both[:K] + (both[K:] + rest)


def exact_dot(left, right, dims):
    return lax.dot_general(
        left, right, dims, precision=HIGHEST, preferred_element_type=jnp.float32
    )


def remote(src, dst, send, recv, where):
    return pltpu.make_async_remote_copy(
        src_ref=src, dst_ref=dst, send_sem=send, recv_sem=recv, device_id=where, device_id_type=MESH
    )


def exchange_kernel(
    inv, rows, cols, count, basis, previous, coupling, energies, tiles_hbm,
    sums_out, applied_out,
    tiles, cstates, rstates, direct, part, ring_in, last, last_in, mid, z_in, msum, m_in, gram, core_in, dim_in,
    tile_sem,
    rg_s, rg_r, z0_s, z0_r, ex_s, ex_r, ag_s, ag_r, rs_s, rs_r, rx_s, rx_r, rz_s, rz_r, mr_s, mr_r,
    co_s, co_r, ar_s, ar_r,
):
    zl, co, y, x, zh = (lax.axis_index(a) for a in AXES)
    me_row = zl * 2 + co
    me_z = zh * 4 + zl
    zo = 1 - zh
    ring_pos = (y, x)
    exch_pos = (x, y)
    ring_axis = ("y", "x")
    exch_axis = ("x", "y")

    def row_id(r):
        return {"zl": r // 2, "co": r % 2}

    def z_id(z):
        return {"zh": z // 4, "zl": z % 4}

    tile_copy = pltpu.make_async_copy(tiles_hbm, tiles, tile_sem)
    tile_copy.start()

    barrier = pltpu.get_barrier_semaphore()

    def hello(where):
        pl.semaphore_signal(barrier, inc=1, device_id=where, device_id_type=MESH)

    for d in range(1, 8):
        hello({"x": (x + d) % 8})
        hello({"y": (y + d) % 8})
        hello(row_id((me_row + d) % 8))
    for d in range(4):
        hello({"zh": zo, "zl": (zl + d) % 4})
    for h in range(2):
        rstates[h, ring_pos[h], zh, exch_pos[h]] = basis[h * HALF : (h + 1) * HALF, :]
    cstates[me_row] = basis[...]
    direct[SLOTS] = jnp.zeros((K, LEN), jnp.float32)
    pl.semaphore_wait(barrier, 25)

    sends = []

    def go(copy):
        copy.start()
        sends.append(copy)

    for h in range(2):
        slot = rstates.at[h, ring_pos[h], zh, exch_pos[h]]
        go(remote(basis.at[pl.ds(h * HALF, HALF)], slot, z0_s.at[h], z0_r.at[h], {"zh": zo}))
    for d in (4, 3, 5, 2, 6, 1, 7):
        for h in range(2):
            slot = rstates.at[h, ring_pos[h], zh, exch_pos[h]]
            go(
                remote(
                    basis.at[pl.ds(h * HALF, HALF)], slot, ex_s.at[h, 0, d], ex_r.at[h, 0, d],
                    {exch_axis[h]: (exch_pos[h] + d) % 8},
                )
            )
    for d in range(1, 8):
        go(remote(basis, cstates.at[me_row], rg_s.at[d], rg_r.at[d], row_id((me_row + d) % 8)))

    def exch_wait(h, c):
        zc = (zh, zo)[c]
        for d in range(1, 8):
            slot = rstates.at[h, ring_pos[h], zc, (exch_pos[h] + 8 - d) % 8]
            remote(slot, slot, ex_s.at[h, c, d], ex_r.at[h, c, d], {exch_axis[h]: exch_pos[h]}).wait_recv()

    def hops(sign, c):
        return 4 if (sign > 0) == (c == 0) else 3

    def ag_copy(h, g, c, s):
        sign = (1, -1)[g]
        zc = (zh, zo)[c]
        slot = rstates.at[h, (ring_pos[h] + 8 - sign * (s - 1)) % 8, zc]
        return remote(
            slot, slot, ag_s.at[h, g, c, s - 1], ag_r.at[h, g, c, s - 1],
            {ring_axis[h]: (ring_pos[h] + 8 + sign) % 8},
        )

    def ag_wait(h, g, c, s):
        sign = (1, -1)[g]
        zc = (zh, zo)[c]
        slot = rstates.at[h, (ring_pos[h] + 8 - sign * s) % 8, zc]
        remote(
            slot, slot, ag_s.at[h, g, c, s - 1], ag_r.at[h, g, c, s - 1],
            {ring_axis[h]: (ring_pos[h] + 8 + sign) % 8},
        ).wait_recv()

    for h in range(2):
        slot = rstates.at[h, ring_pos[h], zo, exch_pos[h]]
        remote(slot, slot, z0_s.at[h], z0_r.at[h], {"zh": zo}).wait_recv()
        for d in (4, 3, 5, 2, 6, 1, 7):
            go(
                remote(
                    slot, slot, ex_s.at[h, 1, d], ex_r.at[h, 1, d],
                    {exch_axis[h]: (exch_pos[h] + d) % 8},
                )
            )
    for h in range(2):
        exch_wait(h, 0)
        for g in range(2):
            go(ag_copy(h, g, 0, 1))

    for d in range(1, 8):
        slot = cstates.at[(me_row + 8 - d) % 8]
        remote(slot, slot, rg_s.at[d], rg_r.at[d], row_id(me_row)).wait_recv()
    tile_copy.wait()
    for s in range(SLOTS):
        direct[s] = dot_three(split(cstates[cols[s]]), split(tiles[s]), NT)
    for h in range(2):
        exch_wait(h, 1)
        for g in range(2):
            go(ag_copy(h, g, 1, 1))

    for a in range(8):
        for b in range(8):
            for z in range(2):
                value = direct[inv[(a * 8 + b) * 2 + z]]
                part[0, a, z, b] = value[:HALF]
                part[1, b, z, a] = value[HALF:]

    def rs_copy(h, g, c, s):
        sign = (1, -1)[g]
        zc = (zo, zh)[c]
        slot = part.at[h, (ring_pos[h] + 8 + sign * (5 - s)) % 8, zc]
        return remote(
            slot, ring_in.at[h, g, c, s - 1], rs_s.at[h, g, c, s - 1], rs_r.at[h, g, c, s - 1],
            {ring_axis[h]: (ring_pos[h] + 8 + sign) % 8},
        )

    def rs_wait(h, g, c, s):
        slot = ring_in.at[h, g, c, s - 1]
        sign = (1, -1)[g]
        remote(
            slot, slot, rs_s.at[h, g, c, s - 1], rs_r.at[h, g, c, s - 1],
            {ring_axis[h]: (ring_pos[h] + 8 + sign) % 8},
        ).wait_recv()

    for c in range(2):
        for h in range(2):
            for g in range(2):
                if hops((1, -1)[g], c) == 4:
                    go(rs_copy(h, g, c, 1))
    for s in range(1, 5):
        for c in range(2):
            for h in range(2):
                for g in range(2):
                    sign = (1, -1)[g]
                    n = hops(sign, c)
                    if s <= n:
                        ag_wait(h, g, c, s)
                        if s < n:
                            go(ag_copy(h, g, c, s + 1))
        for c in range(2):
            zc = (zo, zh)[c]
            for h in range(2):
                for g in range(2):
                    sign = (1, -1)[g]
                    n = hops(sign, c)
                    if n == 4 or s > 1:
                        rs_wait(h, g, c, s)
                    if s < 4:
                        to = (ring_pos[h] + 8 + sign * (4 - s)) % 8
                        if n == 4 or s > 1:
                            part[h, to, zc] = part[h, to, zc] + ring_in[h, g, c, s - 1]
                        go(rs_copy(h, g, c, s + 1))
    for c in range(2):
        zc = (zo, zh)[c]
        for h in range(2):
            last[h, c] = part[h, ring_pos[h], zc] + (ring_in[h, 0, c, 3] + ring_in[h, 1, c, 3])
            for d in (4, 3, 5, 2, 6, 1, 7):
                to = (exch_pos[h] + d) % 8
                go(
                    remote(
                        last.at[h, c, to], last_in.at[h, c, d], rx_s.at[h, c, d], rx_r.at[h, c, d],
                        {exch_axis[h]: to},
                    )
                )

    mirror = []
    for s in range(SLOTS):
        t = rows[s]
        at_y, at_x, at_z = t // 16, (t // 2) % 8, t % 2
        picked = jnp.concatenate([rstates[0, at_y, at_z, at_x], rstates[1, at_x, at_z, at_y]], axis=0)
        mirror.append(dot_three(split(picked), split(tiles[s]), NN))
    live = count[0]
    for u in range(8):
        total = jnp.zeros((K, LEN), jnp.float32)
        for s in range(SLOTS):
            weight = jnp.where((cols[s] == u) & (s < live), 1.0, 0.0)
            total = total + weight * mirror[s]
        msum[u] = total
    for d in (4, 3, 5, 2, 6, 1, 7):
        to = (me_row + d) % 8
        go(remote(msum.at[to], m_in.at[d], mr_s.at[d], mr_r.at[d], row_id(to)))

    halves = []
    for c in range(2):
        for h in range(2):
            total = last[h, c, exch_pos[h]]
            for d in range(1, 8):
                slot = last_in.at[h, c, d]
                remote(slot, slot, rx_s.at[h, c, d], rx_r.at[h, c, d], {exch_axis[h]: exch_pos[h]}).wait_recv()
                total = total + last_in[h, c, d]
            if c == 0:
                mid[h] = total
                go(remote(mid.at[h], z_in.at[h], rz_s.at[h], rz_r.at[h], {"zh": zo}))
            else:
                halves.append(total)
    own_mirror = msum[me_row]
    for d in range(1, 8):
        slot = m_in.at[d]
        remote(slot, slot, mr_s.at[d], mr_r.at[d], row_id(me_row)).wait_recv()
        own_mirror = own_mirror + m_in[d]
    vectors = basis[...]
    applied = energies[...] * vectors + own_mirror - exact_dot(coupling[...], previous[...], NN)
    for h in range(2):
        slot = z_in.at[h]
        remote(slot, slot, rz_s.at[h], rz_r.at[h], {"zh": zo}).wait_recv()
    applied = applied + jnp.concatenate([halves[0] + z_in[0], halves[1] + z_in[1]], axis=0)
    applied_out[...] = applied

    zero = jnp.zeros((K, LEN), jnp.float32)
    total = exact_dot(vectors, jnp.concatenate([applied, zero, vectors, zero], axis=0), NT)
    total = total + exact_dot(applied, jnp.concatenate([zero, applied, zero, zero], axis=0), NT)
    gram[0] = total
    go(remote(gram.at[0], core_in, co_s, co_r, {"co": 1 - co}))
    remote(core_in, core_in, co_s, co_r, {"co": 1 - co}).wait_recv()
    total = total + core_in[...]
    for dim in range(3):
        gram[1 + dim] = total
        for d in (4, 3, 5, 2, 6, 1, 7):
            where = ({"x": (x + d) % 8}, {"y": (y + d) % 8}, z_id((me_z + d) % 8))[dim]
            go(remote(gram.at[1 + dim], dim_in.at[dim, d], ar_s.at[dim, d], ar_r.at[dim, d], where))
        for d in (1, 7, 2, 6, 3, 5, 4):
            slot = dim_in.at[dim, d]
            remote(slot, slot, ar_s.at[dim, d], ar_r.at[dim, d], {"x": x}).wait_recv()
        here = (x, y, me_z)[dim]
        dim_in[dim, 0] = total
        total = dim_in[dim, here]
        for k in range(1, 8):
            total = total + dim_in[dim, (here + 8 - k) % 8]
    sums_out[...] = total
    for copy in sends:
        copy.wait_send()


def finish_kernel(state_count, sums, basis, applied, alpha_out, beta_out, next_out):
    scaled = sums[...] * (1.0 / state_count)
    alpha = scaled[:, :K]
    image = scaled[:, K : 2 * K]
    basis_gram = scaled[:, 2 * K : 3 * K]
    alpha_out[...] = alpha
    alpha_t = alpha.T
    square = exact_dot(alpha_t, alpha, NN)
    projected = exact_dot(alpha_t, exact_dot(basis_gram, alpha, NN), NN)
    gram = image - 2.0 * square + projected
    residual = applied[...] - exact_dot(alpha_t, basis[...], NN)
    at_row = lax.broadcasted_iota(jnp.int32, (K, K), 0)
    at_col = lax.broadcasted_iota(jnp.int32, (K, K), 1)
    eye = jnp.where(at_row == at_col, 1.0, 0.0)
    work = jnp.concatenate([gram, eye], axis=1)
    index = lax.broadcasted_iota(jnp.int32, (K, 2 * K), 0)
    for j in range(K):
        pivot_row = work[j : j + 1, :]
        pivot = work[j : j + 1, j : j + 1]
        scale = 1.0 / jnp.sqrt(pivot)
        row = pivot_row * scale
        column = work[:, j : j + 1] * scale
        work = jnp.where(index > j, work - column * row, jnp.where(index == j, row, work))
    beta_out[...] = jnp.where(at_row <= at_col, work[:, :K], 0.0)
    next_out[...] = exact_dot(work[:, K:], residual, NN)


def shards(basis, previous, coupling, energies, tile_values, tile_rows, tile_cols, counts):
    state_count = basis.shape[1] * lax.axis_size(ROW) * lax.axis_size(COL)
    tiles = tile_values.reshape(SLOTS, LEN, LEN)
    rows = tile_rows.reshape(SLOTS)
    cols = tile_cols.reshape(SLOTS)
    count = counts.reshape(1)
    slot = jnp.arange(SLOTS, dtype=jnp.int32)
    hit = (rows[:, None] == jnp.arange(LEN, dtype=jnp.int32)[None, :]) & (slot < count)[:, None]
    inv = jnp.min(jnp.where(hit, slot[:, None], SLOTS), axis=0)
    f32 = jnp.float32
    vmem = pl.BlockSpec(memory_space=pltpu.VMEM)
    smem = pl.BlockSpec(memory_space=pltpu.SMEM)
    dma = pltpu.SemaphoreType.DMA
    sums, applied = pl.pallas_call(
        exchange_kernel,
        out_shape=(jax.ShapeDtypeStruct((K, LEN), f32), jax.ShapeDtypeStruct((K, LEN), f32)),
        in_specs=[smem, smem, smem, smem, vmem, vmem, vmem, vmem, pl.BlockSpec(memory_space=pl.ANY)],
        out_specs=(vmem, vmem),
        scratch_shapes=[
            pltpu.VMEM((SLOTS, LEN, LEN), f32),
            pltpu.VMEM((8, K, LEN), f32),
            pltpu.VMEM((2, 8, 2, 8, HALF, LEN), f32),
            pltpu.VMEM((SLOTS + 1, K, LEN), f32),
            pltpu.VMEM((2, 8, 2, 8, HALF, LEN), f32),
            pltpu.VMEM((2, 2, 2, 4, 8, HALF, LEN), f32),
            pltpu.VMEM((2, 2, 8, HALF, LEN), f32),
            pltpu.VMEM((2, 2, 8, HALF, LEN), f32),
            pltpu.VMEM((2, HALF, LEN), f32),
            pltpu.VMEM((2, HALF, LEN), f32),
            pltpu.VMEM((8, K, LEN), f32),
            pltpu.VMEM((8, K, LEN), f32),
            pltpu.VMEM((4, K, LEN), f32),
            pltpu.VMEM((K, LEN), f32),
            pltpu.VMEM((3, 8, K, LEN), f32),
            dma(()),
            dma((8,)), dma((8,)),
            dma((2,)), dma((2,)),
            dma((2, 2, 8)), dma((2, 2, 8)),
            dma((2, 2, 2, 4)), dma((2, 2, 2, 4)),
            dma((2, 2, 2, 4)), dma((2, 2, 2, 4)),
            dma((2, 2, 8)), dma((2, 2, 8)),
            dma((2,)), dma((2,)),
            dma((8,)), dma((8,)),
            dma(()), dma(()),
            dma((3, 8)), dma((3, 8)),
        ],
        compiler_params=pltpu.CompilerParams(
            collective_id=0, has_side_effects=True, vmem_limit_bytes=40 * 1024 * 1024
        ),
        name="exchange",
    )(inv, rows, cols, count, basis, previous, coupling, energies.reshape(1, LEN), tiles)
    return pl.pallas_call(
        functools.partial(finish_kernel, state_count),
        out_shape=(
            jax.ShapeDtypeStruct((K, K), f32),
            jax.ShapeDtypeStruct((K, K), f32),
            jax.ShapeDtypeStruct((K, LEN), f32),
        ),
        in_specs=[vmem] * 3,
        out_specs=(vmem, vmem, vmem),
        name="finish",
    )(sums, basis, applied)


def solution(mesh):
    split_mesh = Mesh(mesh.devices.reshape(4, 2, 8, 8, 2), AXES)
    both = ROW + COL
    in_specs = (
        P(None, both),
        P(None, both),
        P(),
        P(both),
        P(ROW, COL, None, None, None),
        P(ROW, COL, None),
        P(ROW, COL, None),
        P(ROW, COL),
    )
    out_specs = (P(), P(), P(None, both))
    return jax.shard_map(
        shards, mesh=split_mesh, in_specs=in_specs, out_specs=out_specs, check_vma=False
    )
```

```python
import functools

import jax
import jax.numpy as jnp
from jax import lax
from jax.experimental import pallas as pl
from jax.experimental.pallas import tpu as pltpu
from jax.sharding import Mesh
from jax.sharding import PartitionSpec as P

AXES = ("zl", "co", "y", "x", "zh")
ROW = ("zl", "co")
COL = ("y", "x", "zh")
K = 32
HALF = 16
LEN = 128
SLOTS = 16
VMEM_LIMIT = 64 * 1024 * 1024 - 65536
RING = 8
MESH = pl.DeviceIdType.MESH
HIGHEST = lax.Precision.HIGHEST
NT = (((1,), (1,)), ((), ()))
NN = (((1,), (0,)), ((), ()))


def split(value):
    high = value.astype(jnp.bfloat16)
    low = (value - high.astype(jnp.float32)).astype(jnp.bfloat16)
    return high, low


def dot_three(left, right, dims):
    lh, ll = left
    rh, rl = right
    both = lax.dot_general(
        jnp.concatenate([lh, ll], axis=0), rh, dims, preferred_element_type=jnp.float32
    )
    rest = lax.dot_general(lh, rl, dims, preferred_element_type=jnp.float32)
    return both[:K] + (both[K:] + rest)


def exact_dot(left, right, dims):
    return lax.dot_general(
        left, right, dims, precision=HIGHEST, preferred_element_type=jnp.float32
    )


def remote(src, dst, send, recv, where):
    return pltpu.make_async_remote_copy(
        src_ref=src, dst_ref=dst, send_sem=send, recv_sem=recv, device_id=where, device_id_type=MESH
    )


def pack(block):
    out = block[:8]
    for q in range(1, 4):
        out = out + pltpu.roll(block[8 * q : 8 * q + 8], 32 * q, 1)
    return out


def unpack(block):
    return jnp.concatenate([block[:, 32 * q : 32 * q + 32] for q in range(4)], axis=0)


def wide(block):
    return jnp.concatenate([block, jnp.zeros((K, LEN - K), jnp.float32)], axis=1)


def finish(state_count, alpha_sum, basis_sum, image_sum, vectors, applied, alpha_out, beta_out, next_out):
    alpha = alpha_sum * (1.0 / state_count)
    basis_gram = basis_sum * (1.0 / state_count)
    alpha_t = alpha.T
    square = exact_dot(alpha_t, alpha, NN)
    projected = exact_dot(alpha_t, exact_dot(basis_gram, alpha, NN), NN)
    residual = applied - exact_dot(alpha_t, vectors, NN)
    alpha_out[...] = alpha
    gram = image_sum() * (1.0 / state_count) - 2.0 * square + projected
    at_row = lax.broadcasted_iota(jnp.int32, (K, K), 0)
    at_col = lax.broadcasted_iota(jnp.int32, (K, K), 1)
    eye = jnp.where(at_row == at_col, 1.0, 0.0)
    work = jnp.concatenate([gram, eye], axis=1)
    index = lax.broadcasted_iota(jnp.int32, (K, 2 * K), 0)
    for j in range(K):
        scale = 1.0 / jnp.sqrt(work[j : j + 1, j : j + 1])
        row = work[j : j + 1, :] * scale
        column = work[:, j : j + 1] * scale
        work = jnp.where(index > j, work - column * row, jnp.where(index == j, row, work))
    beta_out[...] = jnp.where(at_row <= at_col, work[:, :K], 0.0)
    next_out[...] = exact_dot(work[:, K:], residual, NN)


def exchange_kernel(
    state_count,
    rows_hbm, cols_hbm, count_hbm, basis_hbm, previous_hbm, coupling_hbm, energies_hbm, tiles_hbm,
    alpha_out, beta_out, next_out,
    rows, cols, count, inv, inv_lanes, basis, previous, coupling, energies,
    tiles, cstates, rstates, direct, part, ring_in, last, last_in, mid, z_in, msum, m_in,
    early, early_in, early_dim, late, late_in, late_dim,
    in_sem, inv_sem,
    rg_s, rg_r, z0_s, z0_r, ex_s, ex_r, ag_s, ag_r, rs_s, rs_r, rx_s, rx_r, rz_s, rz_r, mr_s, mr_r,
    ec_s, ec_r, er_s, er_r, lc_s, lc_r, lr_s, lr_r,
):
    zl, co, y, x, zh = (lax.axis_index(a) for a in AXES)
    me_row = zl * 2 + co
    me_z = zh * 4 + zl
    zo = 1 - zh
    ring_pos = (y, x)
    exch_pos = (x, y)
    ring_axis = ("y", "x")
    exch_axis = ("x", "y")
    order = (4, 3, 5, 2, 6, 1, 7)

    def row_id(r):
        return {"zl": r // 2, "co": r % 2}

    def z_id(z):
        return {"zh": z // 4, "zl": z % 4}

    barrier = pltpu.get_barrier_semaphore()

    def hello(where):
        pl.semaphore_signal(barrier, inc=1, device_id=where, device_id_type=MESH)

    for d in order:
        hello({"x": (x + d) % 8})
        hello({"y": (y + d) % 8})
        hello(row_id((me_row + d) % 8))
    for d in range(4):
        hello({"zh": zo, "zl": (zl + d) % 4})

    loads = [
        pltpu.make_async_copy(src, dst, in_sem.at[i])
        for i, (src, dst) in enumerate(
            (
                (basis_hbm, basis), (rows_hbm, rows), (count_hbm, count), (cols_hbm, cols), (tiles_hbm, tiles),
                (previous_hbm, previous), (coupling_hbm, coupling), (energies_hbm, energies),
            )
        )
    ]
    for copy in loads:
        copy.start()
    direct[SLOTS] = jnp.zeros((K, LEN), jnp.float32)
    loads[0].wait()
    for h in range(2):
        rstates[h, ring_pos[h], zh, exch_pos[h]] = basis[h * HALF : (h + 1) * HALF, :]
    cstates[me_row] = basis[...]
    loads[1].wait()
    loads[2].wait()
    live = count[0, 0]
    lane = lax.broadcasted_iota(jnp.int32, (8, LEN), 1)
    table = jnp.full((8, LEN), SLOTS, jnp.int32)
    for s in range(SLOTS):
        table = jnp.where(lane == jnp.where(s < live, rows[s], -1), s, table)
    inv_lanes[...] = table
    inv_copy = pltpu.make_async_copy(inv_lanes.at[pl.ds(0, 1)], inv, inv_sem)
    inv_copy.start()
    pl.semaphore_wait(barrier, 25)

    sends = []

    def go(copy):
        copy.start()
        sends.append(copy)

    for h in range(2):
        slot = rstates.at[h, ring_pos[h], zh, exch_pos[h]]
        go(remote(basis.at[pl.ds(h * HALF, HALF)], slot, z0_s.at[h], z0_r.at[h], {"zh": zo}))
    for d in order:
        for h in range(2):
            slot = rstates.at[h, ring_pos[h], zh, exch_pos[h]]
            go(
                remote(
                    basis.at[pl.ds(h * HALF, HALF)], slot, ex_s.at[h, 0, d], ex_r.at[h, 0, d],
                    {exch_axis[h]: (exch_pos[h] + d) % 8},
                )
            )
        go(remote(basis, cstates.at[me_row], rg_s.at[d], rg_r.at[d], row_id((me_row + d) % 8)))

    def exch_wait(h, c):
        zc = (zh, zo)[c]
        for d in range(1, 8):
            slot = rstates.at[h, ring_pos[h], zc, (exch_pos[h] + 8 - d) % 8]
            remote(slot, slot, ex_s.at[h, c, d], ex_r.at[h, c, d], {exch_axis[h]: exch_pos[h]}).wait_recv()

    def hops(sign, c):
        return 4 if (sign > 0) == (c == 0) else 3

    def ag_copy(h, g, c, s):
        sign = (1, -1)[g]
        zc = (zh, zo)[c]
        slot = rstates.at[h, (ring_pos[h] + 8 - sign * (s - 1)) % 8, zc]
        return remote(
            slot, slot, ag_s.at[h, g, c, s - 1], ag_r.at[h, g, c, s - 1],
            {ring_axis[h]: (ring_pos[h] + 8 + sign) % 8},
        )

    def ag_wait(h, g, c, s):
        sign = (1, -1)[g]
        zc = (zh, zo)[c]
        slot = rstates.at[h, (ring_pos[h] + 8 - sign * s) % 8, zc]
        remote(
            slot, slot, ag_s.at[h, g, c, s - 1], ag_r.at[h, g, c, s - 1],
            {ring_axis[h]: (ring_pos[h] + 8 + sign) % 8},
        ).wait_recv()

    for h in range(2):
        slot = rstates.at[h, ring_pos[h], zo, exch_pos[h]]
        remote(slot, slot, z0_s.at[h], z0_r.at[h], {"zh": zo}).wait_recv()
        for d in order:
            go(
                remote(
                    slot, slot, ex_s.at[h, 1, d], ex_r.at[h, 1, d],
                    {exch_axis[h]: (exch_pos[h] + d) % 8},
                )
            )
    for h in range(2):
        exch_wait(h, 0)
        for g in range(2):
            go(ag_copy(h, g, 0, 1))

    for d in range(1, 8):
        slot = cstates.at[(me_row + 8 - d) % 8]
        remote(slot, slot, rg_s.at[d], rg_r.at[d], row_id(me_row)).wait_recv()
    for copy in loads[3:]:
        copy.wait()
    inv_copy.wait()
    for s in range(SLOTS):
        direct[s] = dot_three(split(cstates[cols[s]]), split(tiles[s]), NT)
    for h in range(2):
        exch_wait(h, 1)
        for g in range(2):
            go(ag_copy(h, g, 1, 1))

    for a in range(8):
        for b in range(8):
            for z in range(2):
                value = direct[inv[0, (a * 8 + b) * 2 + z]]
                part[0, a, z, b] = value[:HALF]
                part[1, b, z, a] = value[HALF:]

    def rs_copy(h, g, c, s):
        sign = (1, -1)[g]
        zc = (zo, zh)[c]
        slot = part.at[h, (ring_pos[h] + 8 + sign * (5 - s)) % 8, zc]
        return remote(
            slot, ring_in.at[h, g, c, s - 1], rs_s.at[h, g, c, s - 1], rs_r.at[h, g, c, s - 1],
            {ring_axis[h]: (ring_pos[h] + 8 + sign) % 8},
        )

    def rs_wait(h, g, c, s):
        slot = ring_in.at[h, g, c, s - 1]
        sign = (1, -1)[g]
        remote(
            slot, slot, rs_s.at[h, g, c, s - 1], rs_r.at[h, g, c, s - 1],
            {ring_axis[h]: (ring_pos[h] + 8 + sign) % 8},
        ).wait_recv()

    def rs_step(c, s):
        zc = (zo, zh)[c]
        for h in range(2):
            for g in range(2):
                sign = (1, -1)[g]
                n = hops(sign, c)
                if s == 0:
                    if n == 4:
                        go(rs_copy(h, g, c, 1))
                    continue
                if n == 4 or s > 1:
                    rs_wait(h, g, c, s)
                if s < 4:
                    to = (ring_pos[h] + 8 + sign * (4 - s)) % 8
                    if n == 4 or s > 1:
                        part[h, to, zc] = part[h, to, zc] + ring_in[h, g, c, s - 1]
                    go(rs_copy(h, g, c, s + 1))

    def rs_last(c):
        zc = (zo, zh)[c]
        for h in range(2):
            last[h, c] = part[h, ring_pos[h], zc] + (ring_in[h, 0, c, 3] + ring_in[h, 1, c, 3])
            for d in order:
                to = (exch_pos[h] + d) % 8
                go(
                    remote(
                        last.at[h, c, to], last_in.at[h, c, d], rx_s.at[h, c, d], rx_r.at[h, c, d],
                        {exch_axis[h]: to},
                    )
                )

    def ag_step(s):
        for c in range(2):
            for h in range(2):
                for g in range(2):
                    n = hops((1, -1)[g], c)
                    if s <= n:
                        ag_wait(h, g, c, s)
                        if s < n:
                            go(ag_copy(h, g, c, s + 1))

    rs_step(0, 0)
    for s in range(1, 5):
        ag_step(s)
        rs_step(1, s - 1)
        rs_step(0, s)
    rs_last(0)
    rs_step(1, 4)
    rs_last(1)

    mirror = []
    row_parts = []
    for s in range(SLOTS):
        t = rows[s]
        at_y, at_x, at_z = t // 16, (t // 2) % 8, t % 2
        picked = split(
            jnp.concatenate([rstates[0, at_y, at_z, at_x], rstates[1, at_x, at_z, at_y]], axis=0)
        )
        row_parts.append(picked)
        mirror.append(dot_three(picked, split(tiles[s]), NN))
    for u in range(8):
        total = jnp.zeros((K, LEN), jnp.float32)
        for s in range(SLOTS):
            weight = jnp.where((cols[s] == u) & (s < live), 1.0, 0.0)
            total = total + weight * mirror[s]
        msum[u] = total
    for d in order:
        to = (me_row + d) % 8
        go(remote(msum.at[to], m_in.at[d], mr_s.at[d], mr_r.at[d], row_id(to)))

    vectors = basis[...]
    own = energies[...] * vectors - exact_dot(coupling[...], previous[...], NN)
    live_direct = [split(jnp.where(s < live, 1.0, 0.0) * direct[s]) for s in range(SLOTS)]
    rh = jnp.concatenate([p[0] for p in row_parts], axis=1)
    rl = jnp.concatenate([p[1] for p in row_parts], axis=1)
    dh = jnp.concatenate([p[0] for p in live_direct], axis=1)
    dl = jnp.concatenate([p[1] for p in live_direct], axis=1)
    cross = lax.dot_general(jnp.concatenate([rh, rl], axis=0), dh, NT, preferred_element_type=jnp.float32)
    cross = cross[:K] + (cross[K:] + lax.dot_general(rh, dl, NT, preferred_element_type=jnp.float32))
    cross = cross + cross.T + exact_dot(vectors, own, NT)
    early[0, :8] = pack(wide(cross))
    early[0, 8:] = pack(wide(exact_dot(vectors, vectors, NT)))

    def core_start(src, dst, send, recv):
        go(remote(src, dst, send, recv, {"co": 1 - co}))

    def core_wait(dst, send, recv):
        remote(dst, dst, send, recv, {"co": 1 - co}).wait_recv()

    def dim_start(dim, src, dst, send, recv):
        for d in order:
            where = ({"x": (x + d) % 8}, {"y": (y + d) % 8}, z_id((me_z + d) % 8))[dim]
            go(remote(src, dst.at[dim, d], send.at[dim, d], recv.at[dim, d], where))

    def dim_wait(dim, mine, dst, send, recv):
        for d in range(1, 8):
            slot = dst.at[dim, d]
            remote(slot, slot, send.at[dim, d], recv.at[dim, d], {"x": x}).wait_recv()
        dst[dim, 0] = mine
        here = (x, y, me_z)[dim]
        total = dst[dim, here]
        for k in range(1, 8):
            total = total + dst[dim, (here + 8 - k) % 8]
        return total

    core_start(early.at[0], early_in, ec_s, ec_r)

    halves = []
    for c in range(2):
        for h in range(2):
            total = last[h, c, exch_pos[h]]
            for d in range(1, 8):
                slot = last_in.at[h, c, d]
                remote(slot, slot, rx_s.at[h, c, d], rx_r.at[h, c, d], {exch_axis[h]: exch_pos[h]}).wait_recv()
                total = total + last_in[h, c, d]
            if c == 0:
                mid[h] = total
                go(remote(mid.at[h], z_in.at[h], rz_s.at[h], rz_r.at[h], {"zh": zo}))
            else:
                halves.append(total)
    core_wait(early_in, ec_s, ec_r)
    early[1] = early[0] + early_in[...]
    dim_start(0, early.at[1], early_dim, er_s, er_r)
    for d in range(1, 8):
        slot = m_in.at[d]
        remote(slot, slot, mr_s.at[d], mr_r.at[d], row_id(me_row)).wait_recv()
    applied = own + msum[me_row]
    for d in range(1, 8):
        applied = applied + m_in[d]
    for h in range(2):
        slot = z_in.at[h]
        remote(slot, slot, rz_s.at[h], rz_r.at[h], {"zh": zo}).wait_recv()
    applied = applied + jnp.concatenate([halves[0] + z_in[0], halves[1] + z_in[1]], axis=0)

    late[0] = pack(wide(exact_dot(applied, applied, NT)))
    core_start(late.at[0], late_in, lc_s, lc_r)
    early[2] = dim_wait(0, early[1], early_dim, er_s, er_r)
    dim_start(1, early.at[2], early_dim, er_s, er_r)
    core_wait(late_in, lc_s, lc_r)
    late[1] = late[0] + late_in[...]
    dim_start(0, late.at[1], late_dim, lr_s, lr_r)
    early[3] = dim_wait(1, early[2], early_dim, er_s, er_r)
    dim_start(2, early.at[3], early_dim, er_s, er_r)
    late[2] = dim_wait(0, late[1], late_dim, lr_s, lr_r)
    dim_start(1, late.at[2], late_dim, lr_s, lr_r)
    sums = dim_wait(2, early[3], early_dim, er_s, er_r)
    late[3] = dim_wait(1, late[2], late_dim, lr_s, lr_r)
    dim_start(2, late.at[3], late_dim, lr_s, lr_r)
    finish(
        state_count, unpack(sums[:8]), unpack(sums[8:]),
        lambda: unpack(dim_wait(2, late[3], late_dim, lr_s, lr_r)),
        vectors, applied, alpha_out, beta_out, next_out,
    )
    for copy in sends:
        copy.wait_send()


def shards(basis, previous, coupling, energies, tile_values, tile_rows, tile_cols, counts):
    state_count = basis.shape[1] * lax.axis_size(ROW) * lax.axis_size(COL)
    f32, i32 = jnp.float32, jnp.int32
    vmem = pl.BlockSpec(memory_space=pltpu.VMEM)
    dma = pltpu.SemaphoreType.DMA
    return pl.pallas_call(
        functools.partial(exchange_kernel, state_count),
        out_shape=(
            jax.ShapeDtypeStruct((K, K), f32),
            jax.ShapeDtypeStruct((K, K), f32),
            jax.ShapeDtypeStruct((K, LEN), f32),
        ),
        in_specs=[pl.BlockSpec(memory_space=pl.ANY)] * 8,
        out_specs=(vmem, vmem, vmem),
        scratch_shapes=[
            pltpu.SMEM((SLOTS,), i32),
            pltpu.SMEM((SLOTS,), i32),
            pltpu.SMEM((1, 1), i32),
            pltpu.SMEM((1, LEN), i32),
            pltpu.VMEM((8, LEN), i32),
            pltpu.VMEM((K, LEN), f32),
            pltpu.VMEM((K, LEN), f32),
            pltpu.VMEM((K, K), f32),
            pltpu.VMEM((1, LEN), f32),
            pltpu.VMEM((SLOTS, LEN, LEN), f32),
            pltpu.VMEM((8, K, LEN), f32),
            pltpu.VMEM((2, 8, 2, 8, HALF, LEN), f32),
            pltpu.VMEM((SLOTS + 1, K, LEN), f32),
            pltpu.VMEM((2, 8, 2, 8, HALF, LEN), f32),
            pltpu.VMEM((2, 2, 2, 4, 8, HALF, LEN), f32),
            pltpu.VMEM((2, 2, 8, HALF, LEN), f32),
            pltpu.VMEM((2, 2, 8, HALF, LEN), f32),
            pltpu.VMEM((2, HALF, LEN), f32),
            pltpu.VMEM((2, HALF, LEN), f32),
            pltpu.VMEM((8, K, LEN), f32),
            pltpu.VMEM((8, K, LEN), f32),
            pltpu.VMEM((4, 16, LEN), f32),
            pltpu.VMEM((16, LEN), f32),
            pltpu.VMEM((3, 8, 16, LEN), f32),
            pltpu.VMEM((4, 8, LEN), f32),
            pltpu.VMEM((8, LEN), f32),
            pltpu.VMEM((3, 8, 8, LEN), f32),
            dma((8,)), dma(()),
            dma((8,)), dma((8,)),
            dma((2,)), dma((2,)),
            dma((2, 2, 8)), dma((2, 2, 8)),
            dma((2, 2, 2, 4)), dma((2, 2, 2, 4)),
            dma((2, 2, 2, 4)), dma((2, 2, 2, 4)),
            dma((2, 2, 8)), dma((2, 2, 8)),
            dma((2,)), dma((2,)),
            dma((8,)), dma((8,)),
            dma(()), dma(()),
            dma((3, 8)), dma((3, 8)),
            dma(()), dma(()),
            dma((3, 8)), dma((3, 8)),
        ],
        compiler_params=pltpu.CompilerParams(
            collective_id=0, has_side_effects=True, vmem_limit_bytes=VMEM_LIMIT
        ),
        name="exchange",
    )(
        tile_rows.reshape(SLOTS), tile_cols.reshape(SLOTS), counts, basis, previous, coupling,
        energies.reshape(1, LEN), tile_values.reshape(SLOTS, LEN, LEN),
    )


def solution(mesh):
    split_mesh = Mesh(mesh.devices.reshape(4, 2, 8, 8, 2), AXES)
    both = ROW + COL
    in_specs = (
        P(None, both),
        P(None, both),
        P(),
        P(both),
        P(ROW, COL, None, None, None),
        P(ROW, COL, None),
        P(ROW, COL, None),
        P(ROW, COL),
    )
    out_specs = (P(), P(), P(None, both))
    return jax.shard_map(
        shards, mesh=split_mesh, in_specs=in_specs, out_specs=out_specs, check_vma=False
    )
```

```python
import functools

import jax
import jax.numpy as jnp
from jax import lax
from jax.experimental import pallas as pl
from jax.experimental.pallas import tpu as pltpu
from jax.sharding import Mesh
from jax.sharding import PartitionSpec as P

AXES = ("zl", "co", "y", "x", "zh")
ROW = ("zl", "co")
COL = ("y", "x", "zh")
K = 32
HALF = 16
LEN = 128
SLOTS = 16
VMEM_LIMIT = 64 * 1024 * 1024 - 65536
RING = 8
MESH = pl.DeviceIdType.MESH
HIGHEST = lax.Precision.HIGHEST
NT = (((1,), (1,)), ((), ()))
NN = (((1,), (0,)), ((), ()))


def split(value):
    high = value.astype(jnp.bfloat16)
    low = (value - high.astype(jnp.float32)).astype(jnp.bfloat16)
    return high, low


def dot_three(left, right, dims):
    lh, ll = left
    rh, rl = right
    both = lax.dot_general(
        jnp.concatenate([lh, ll], axis=0), rh, dims, preferred_element_type=jnp.float32
    )
    rest = lax.dot_general(lh, rl, dims, preferred_element_type=jnp.float32)
    return both[:K] + (both[K:] + rest)


def exact_dot(left, right, dims):
    return lax.dot_general(
        left, right, dims, precision=HIGHEST, preferred_element_type=jnp.float32
    )


def remote(src, dst, send, recv, where):
    return pltpu.make_async_remote_copy(
        src_ref=src, dst_ref=dst, send_sem=send, recv_sem=recv, device_id=where, device_id_type=MESH
    )


def pack(block):
    out = block[:8]
    for q in range(1, 4):
        out = out + pltpu.roll(block[8 * q : 8 * q + 8], 32 * q, 1)
    return out


def unpack(block):
    return jnp.concatenate([block[:, 32 * q : 32 * q + 32] for q in range(4)], axis=0)


def wide(block):
    return jnp.concatenate([block, jnp.zeros((K, LEN - K), jnp.float32)], axis=1)


def finish(state_count, alpha_sum, basis_sum, image_sum, vectors, applied, alpha_out, beta_out, next_out):
    alpha = alpha_sum * (1.0 / state_count)
    basis_gram = basis_sum * (1.0 / state_count)
    alpha_t = alpha.T
    square = exact_dot(alpha_t, alpha, NN)
    projected = exact_dot(alpha_t, exact_dot(basis_gram, alpha, NN), NN)
    residual = applied - exact_dot(alpha_t, vectors, NN)
    alpha_out[...] = alpha
    gram = image_sum() * (1.0 / state_count) - 2.0 * square + projected
    upper, inverse = factor(gram)
    beta_out[...] = upper
    next_out[...] = exact_dot(inverse, residual, NN)


def factor(gram):
    at_row = lax.broadcasted_iota(jnp.int32, (K, K), 0)
    at_col = lax.broadcasted_iota(jnp.int32, (K, K), 1)
    work = jnp.concatenate([gram, jnp.where(at_row == at_col, 1.0, 0.0)], axis=1)
    done = []
    sub = lax.broadcasted_iota(jnp.int32, (8, 2 * K), 0)
    for q in range(4):
        block = work[:8]
        rest = work[8:]
        left = 24 - 8 * q
        heads = [jnp.broadcast_to(block[:, 8 * q + k : 8 * q + k + 1], (8, 2 * K)) for k in range(8)]
        rows = [jnp.broadcast_to(block[k : k + 1, :], (8, 2 * K)) for k in range(8)]
        full = {}
        for k in range(8):
            for m in range(k, 8):
                full[k, m] = jnp.broadcast_to(heads[m][k : k + 1, :], (8, 2 * K))
        if left:
            cols = [
                jnp.broadcast_to(rest[:, 8 * q + k : 8 * q + k + 1], (left, 2 * K)).reshape(left // 8, 8, 2 * K)
                for k in range(8)
            ]
            rest = rest.reshape(left // 8, 8, 2 * K)
        out = jnp.zeros((8, 2 * K), jnp.float32)
        for k in range(8):
            pivot = full[k, k]
            scale = 1.0 / pivot
            root = lax.rsqrt(pivot)
            root = root * (1.5 - 0.5 * pivot * root * root)
            out = jnp.where(sub == k, rows[k] * root, out)
            factors = {m: full[k, m] * scale for m in range(k + 1, 8)}
            for m in range(k + 1, 8):
                for n in range(m, 8):
                    full[m, n] = full[m, n] - full[k, n] * factors[m]
            for m in range(k + 1, 8):
                rows[m] = rows[m] - rows[k] * factors[m]
            if left:
                rest = rest - cols[k] * (rows[k] * scale)[None]
                for m in range(k + 1, 8):
                    cols[m] = cols[m] - cols[k] * factors[m][None]
        done.append(out)
        if left:
            work = rest.reshape(left, 2 * K)
    both = jnp.concatenate(done, axis=0)
    return jnp.where(at_row <= at_col, both[:, :K], 0.0), both[:, K:]


def exchange_kernel(
    state_count,
    rows_hbm, cols_hbm, count_hbm, basis_hbm, previous_hbm, coupling_hbm, energies_hbm, tiles_hbm,
    out,
    rows, cols, count, inv, inv_lanes, basis, previous, coupling, energies,
    tiles, cstates, rstates, direct, part, ring_in, last, last_in, mid, z_in, msum, m_in,
    early, early_in, early_dim, late, late_in, late_dim,
    in_sem, inv_sem,
    rg_s, rg_r, z0_s, z0_r, ex_s, ex_r, ag_s, ag_r, rs_s, rs_r, rx_s, rx_r, rz_s, rz_r, mr_s, mr_r,
    ec_s, ec_r, er_s, er_r, lc_s, lc_r, lr_s, lr_r,
):
    zl, co, y, x, zh = (lax.axis_index(a) for a in AXES)
    me_row = zl * 2 + co
    me_z = zh * 4 + zl
    zo = 1 - zh
    ring_pos = (y, x)
    exch_pos = (x, y)
    ring_axis = ("y", "x")
    exch_axis = ("x", "y")
    order = (4, 3, 5, 2, 6, 1, 7)

    def row_id(r):
        return {"zl": lax.div(r, 2), "co": lax.rem(r, 2)}

    def z_id(z):
        return {"zh": lax.div(z, 4), "zl": lax.rem(z, 4)}

    loads = [
        pltpu.make_async_copy(src, dst, in_sem.at[i])
        for i, (src, dst) in enumerate(
            (
                (basis_hbm, basis), (rows_hbm, rows), (count_hbm, count), (cols_hbm, cols), (tiles_hbm, tiles),
                (previous_hbm, previous), (coupling_hbm, coupling), (energies_hbm, energies),
            )
        )
    ]
    loads[0].start()
    barrier = pltpu.get_barrier_semaphore()

    def hello(where):
        pl.semaphore_signal(barrier, inc=1, device_id=where, device_id_type=MESH)

    for d in order:
        hello({"x": lax.rem(x + d, 8)})
        hello({"y": lax.rem(y + d, 8)})
        hello(row_id(lax.rem(me_row + d, 8)))
    for d in range(4):
        hello({"zh": zo, "zl": lax.rem(zl + d, 4)})

    for copy in loads[1:]:
        copy.start()
    direct[SLOTS] = jnp.zeros((K, LEN), jnp.float32)
    loads[0].wait()
    for h in range(2):
        rstates[h, ring_pos[h], zh, exch_pos[h]] = basis[h * HALF : (h + 1) * HALF, :]
    cstates[me_row] = basis[...]
    pl.semaphore_wait(barrier, 25)

    sends = []

    def go(copy):
        copy.start()
        sends.append(copy)

    for h in range(2):
        slot = rstates.at[h, ring_pos[h], zh, exch_pos[h]]
        go(remote(basis.at[pl.ds(h * HALF, HALF)], slot, z0_s.at[h], z0_r.at[h], {"zh": zo}))
    for d in order:
        for h in range(2):
            slot = rstates.at[h, ring_pos[h], zh, exch_pos[h]]
            go(
                remote(
                    basis.at[pl.ds(h * HALF, HALF)], slot, ex_s.at[h, 0, d], ex_r.at[h, 0, d],
                    {exch_axis[h]: lax.rem(exch_pos[h] + d, 8)},
                )
            )
        go(remote(basis, cstates.at[me_row], rg_s.at[d], rg_r.at[d], row_id(lax.rem(me_row + d, 8))))

    loads[1].wait()
    loads[2].wait()
    live = count[0, 0]
    lane = lax.broadcasted_iota(jnp.int32, (8, LEN), 1)
    table = jnp.full((8, LEN), SLOTS, jnp.int32)
    for s in range(SLOTS):
        table = jnp.where(lane == jnp.where(s < live, rows[s], -1), s, table)
    inv_lanes[...] = table
    inv_copy = pltpu.make_async_copy(inv_lanes.at[pl.ds(0, 1)], inv, inv_sem)
    inv_copy.start()

    def exch_wait(h, c):
        zc = (zh, zo)[c]
        for d in range(1, 8):
            slot = rstates.at[h, ring_pos[h], zc, lax.rem(exch_pos[h] + 8 - d, 8)]
            remote(slot, slot, ex_s.at[h, c, d], ex_r.at[h, c, d], {exch_axis[h]: exch_pos[h]}).wait_recv()

    def hops(sign, c):
        return 4 if (sign > 0) == (c == 0) else 3

    def ag_copy(h, g, c, s):
        sign = (1, -1)[g]
        zc = (zh, zo)[c]
        slot = rstates.at[h, lax.rem(ring_pos[h] + 8 - sign * (s - 1), 8), zc]
        return remote(
            slot, slot, ag_s.at[h, g, c, s - 1], ag_r.at[h, g, c, s - 1],
            {ring_axis[h]: lax.rem(ring_pos[h] + 8 + sign, 8)},
        )

    def ag_wait(h, g, c, s):
        sign = (1, -1)[g]
        zc = (zh, zo)[c]
        slot = rstates.at[h, lax.rem(ring_pos[h] + 8 - sign * s, 8), zc]
        remote(
            slot, slot, ag_s.at[h, g, c, s - 1], ag_r.at[h, g, c, s - 1],
            {ring_axis[h]: lax.rem(ring_pos[h] + 8 + sign, 8)},
        ).wait_recv()

    for h in range(2):
        slot = rstates.at[h, ring_pos[h], zo, exch_pos[h]]
        remote(slot, slot, z0_s.at[h], z0_r.at[h], {"zh": zo}).wait_recv()
        for d in order:
            go(
                remote(
                    slot, slot, ex_s.at[h, 1, d], ex_r.at[h, 1, d],
                    {exch_axis[h]: lax.rem(exch_pos[h] + d, 8)},
                )
            )
    for h in range(2):
        exch_wait(h, 0)
        for g in range(2):
            go(ag_copy(h, g, 0, 1))

    for d in range(1, 8):
        slot = cstates.at[lax.rem(me_row + 8 - d, 8)]
        remote(slot, slot, rg_s.at[d], rg_r.at[d], row_id(me_row)).wait_recv()
    for copy in loads[3:]:
        copy.wait()
    inv_copy.wait()
    for s in range(SLOTS):
        direct[s] = dot_three(split(cstates[cols[s]]), split(tiles[s]), NT)
    for h in range(2):
        exch_wait(h, 1)
        for g in range(2):
            go(ag_copy(h, g, 1, 1))

    for a in range(8):
        for b in range(8):
            for z in range(2):
                value = direct[inv[0, (a * 8 + b) * 2 + z]]
                part[0, a, z, b] = value[:HALF]
                part[1, b, z, a] = value[HALF:]

    def rs_copy(h, g, c, s):
        sign = (1, -1)[g]
        zc = (zo, zh)[c]
        slot = part.at[h, lax.rem(ring_pos[h] + 8 + sign * (5 - s), 8), zc]
        return remote(
            slot, ring_in.at[h, g, c, s - 1], rs_s.at[h, g, c, s - 1], rs_r.at[h, g, c, s - 1],
            {ring_axis[h]: lax.rem(ring_pos[h] + 8 + sign, 8)},
        )

    def rs_wait(h, g, c, s):
        slot = ring_in.at[h, g, c, s - 1]
        sign = (1, -1)[g]
        remote(
            slot, slot, rs_s.at[h, g, c, s - 1], rs_r.at[h, g, c, s - 1],
            {ring_axis[h]: lax.rem(ring_pos[h] + 8 + sign, 8)},
        ).wait_recv()

    def rs_step(c, s):
        zc = (zo, zh)[c]
        for h in range(2):
            for g in range(2):
                sign = (1, -1)[g]
                n = hops(sign, c)
                if s == 0:
                    if n == 4:
                        go(rs_copy(h, g, c, 1))
                    continue
                if n == 4 or s > 1:
                    rs_wait(h, g, c, s)
                if s < 4:
                    to = lax.rem(ring_pos[h] + 8 + sign * (4 - s), 8)
                    if n == 4 or s > 1:
                        part[h, to, zc] = part[h, to, zc] + ring_in[h, g, c, s - 1]
                    go(rs_copy(h, g, c, s + 1))

    def rs_last(c):
        zc = (zo, zh)[c]
        for h in range(2):
            last[h, c] = part[h, ring_pos[h], zc] + (ring_in[h, 0, c, 3] + ring_in[h, 1, c, 3])
            for d in order:
                to = lax.rem(exch_pos[h] + d, 8)
                go(
                    remote(
                        last.at[h, c, to], last_in.at[h, c, d], rx_s.at[h, c, d], rx_r.at[h, c, d],
                        {exch_axis[h]: to},
                    )
                )

    def ag_flow(c, s):
        for h in range(2):
            for g in range(2):
                n = hops((1, -1)[g], c)
                if s <= n:
                    ag_wait(h, g, c, s)
                    if s < n:
                        go(ag_copy(h, g, c, s + 1))

    mirror = []
    row_parts = []

    def mirror_step(tiles_from, tiles_to):
        for s in range(tiles_from, tiles_to):
            t = rows[s]
            at_y, at_x, at_z = lax.div(t, 16), lax.rem(lax.div(t, 2), 8), lax.rem(t, 2)
            picked = split(
                jnp.concatenate([rstates[0, at_y, at_z, at_x], rstates[1, at_x, at_z, at_y]], axis=0)
            )
            row_parts.append(picked)
            mirror.append(dot_three(picked, split(tiles[s]), NN))

    def drain():
        while sends:
            sends.pop(0).wait_send()

    rs_step(0, 0)
    ag_flow(0, 1)
    rs_step(1, 0)
    rs_step(0, 1)
    ag_flow(1, 1)
    for s in range(2, 5):
        ag_flow(0, s)
        rs_step(0, s)
        if s == 4:
            rs_last(0)
        rs_step(1, s - 1)
        ag_flow(1, s)
    mirror_step(0, 8)
    rs_step(1, 4)
    rs_last(1)
    mirror_step(8, SLOTS)
    weights = [[jnp.where((cols[s] == u) & (s < live), 1.0, 0.0) for s in range(SLOTS)] for u in range(8)]
    for u in range(8):
        total = weights[u][0] * mirror[0]
        for s in range(1, SLOTS):
            total = total + weights[u][s] * mirror[s]
        msum[u] = total
    for d in order:
        to = lax.rem(me_row + d, 8)
        go(remote(msum.at[to], m_in.at[d], mr_s.at[d], mr_r.at[d], row_id(to)))

    def last_sum(c, h):
        total = last[h, c, exch_pos[h]]
        for d in range(1, 8):
            slot = last_in.at[h, c, d]
            remote(slot, slot, rx_s.at[h, c, d], rx_r.at[h, c, d], {exch_axis[h]: exch_pos[h]}).wait_recv()
            total = total + last_in[h, c, d]
        return total

    for h in range(2):
        mid[h] = last_sum(0, h)
        go(remote(mid.at[h], z_in.at[h], rz_s.at[h], rz_r.at[h], {"zh": zo}))

    def core_start(src, dst, send, recv):
        go(remote(src, dst, send, recv, {"co": 1 - co}))

    def core_wait(dst, send, recv):
        remote(dst, dst, send, recv, {"co": 1 - co}).wait_recv()

    def dim_start(dim, src, dst, send, recv):
        for d in order:
            where = ({"x": lax.rem(x + d, 8)}, {"y": lax.rem(y + d, 8)}, z_id(lax.rem(me_z + d, 8)))[dim]
            go(remote(src, dst.at[dim, d], send.at[dim, d], recv.at[dim, d], where))

    def dim_wait(dim, mine, dst, send, recv):
        for d in range(1, 8):
            slot = dst.at[dim, d]
            remote(slot, slot, send.at[dim, d], recv.at[dim, d], {"x": x}).wait_recv()
        dst[dim, 0] = mine
        here = (x, y, me_z)[dim]
        total = dst[dim, here]
        for k in range(1, 8):
            total = total + dst[dim, lax.rem(here + 8 - k, 8)]
        return total

    vectors = basis[...]
    own = energies[...] * vectors - exact_dot(coupling[...], previous[...], NN)
    live_direct = [split(jnp.where(s < live, 1.0, 0.0) * direct[s]) for s in range(SLOTS)]
    rh = jnp.concatenate([p[0] for p in row_parts], axis=1)
    rl = jnp.concatenate([p[1] for p in row_parts], axis=1)
    dh = jnp.concatenate([p[0] for p in live_direct], axis=1)
    dl = jnp.concatenate([p[1] for p in live_direct], axis=1)
    cross = lax.dot_general(jnp.concatenate([rh, rl], axis=0), dh, NT, preferred_element_type=jnp.float32)
    cross = cross[:K] + (cross[K:] + lax.dot_general(rh, dl, NT, preferred_element_type=jnp.float32))
    cross = cross + cross.T + exact_dot(vectors, own, NT)
    early[0, :8] = pack(wide(cross))
    early[0, 8:] = pack(wide(exact_dot(vectors, vectors, NT)))
    core_start(early.at[0], early_in, ec_s, ec_r)
    halves = [last_sum(1, h) for h in range(2)]
    core_wait(early_in, ec_s, ec_r)
    early[1] = early[0] + early_in[...]
    dim_start(0, early.at[1], early_dim, er_s, er_r)
    for d in range(1, 8):
        slot = m_in.at[d]
        remote(slot, slot, mr_s.at[d], mr_r.at[d], row_id(me_row)).wait_recv()
    applied = own + msum[me_row]
    for d in range(1, 8):
        applied = applied + m_in[d]
    for h in range(2):
        slot = z_in.at[h]
        remote(slot, slot, rz_s.at[h], rz_r.at[h], {"zh": zo}).wait_recv()
    applied = applied + jnp.concatenate([halves[0] + z_in[0], halves[1] + z_in[1]], axis=0)

    late[0] = pack(wide(exact_dot(applied, applied, NT)))
    core_start(late.at[0], late_in, lc_s, lc_r)
    core_wait(late_in, lc_s, lc_r)
    late[1] = late[0] + late_in[...]
    dim_start(0, late.at[1], late_dim, lr_s, lr_r)
    early[2] = dim_wait(0, early[1], early_dim, er_s, er_r)
    dim_start(1, early.at[2], early_dim, er_s, er_r)
    late[2] = dim_wait(0, late[1], late_dim, lr_s, lr_r)
    dim_start(1, late.at[2], late_dim, lr_s, lr_r)
    early[3] = dim_wait(1, early[2], early_dim, er_s, er_r)
    dim_start(2, early.at[3], early_dim, er_s, er_r)
    drain()
    late[3] = dim_wait(1, late[2], late_dim, lr_s, lr_r)
    dim_start(2, late.at[3], late_dim, lr_s, lr_r)
    sums = dim_wait(2, early[3], early_dim, er_s, er_r)
    finish(
        state_count, unpack(sums[:8]), unpack(sums[8:]),
        lambda: unpack(dim_wait(2, late[3], late_dim, lr_s, lr_r)),
        vectors, applied, out.at[pl.ds(K, K), pl.ds(0, K)], out.at[pl.ds(2 * K, K), pl.ds(0, K)], out.at[pl.ds(0, K)],
    )
    drain()


def deliver_kernel(packed, alpha_out, beta_out, next_out):
    next_out[...] = packed[:K, :]
    alpha_out[...] = packed[K : 2 * K, :K]
    beta_out[...] = packed[2 * K :, :K]


def shards(basis, previous, coupling, energies, tile_values, tile_rows, tile_cols, counts):
    state_count = basis.shape[1] * lax.axis_size(ROW) * lax.axis_size(COL)
    f32, i32 = jnp.float32, jnp.int32
    vmem = pl.BlockSpec(memory_space=pltpu.VMEM)
    dma = pltpu.SemaphoreType.DMA
    out = pl.pallas_call(
        functools.partial(exchange_kernel, state_count),
        out_shape=jax.ShapeDtypeStruct((3 * K, LEN), f32),
        in_specs=[pl.BlockSpec(memory_space=pl.ANY)] * 8,
        out_specs=vmem,
        scratch_shapes=[
            pltpu.SMEM((SLOTS,), i32),
            pltpu.SMEM((SLOTS,), i32),
            pltpu.SMEM((1, 1), i32),
            pltpu.SMEM((1, LEN), i32),
            pltpu.VMEM((8, LEN), i32),
            pltpu.VMEM((K, LEN), f32),
            pltpu.VMEM((K, LEN), f32),
            pltpu.VMEM((K, K), f32),
            pltpu.VMEM((1, LEN), f32),
            pltpu.VMEM((SLOTS, LEN, LEN), f32),
            pltpu.VMEM((8, K, LEN), f32),
            pltpu.VMEM((2, 8, 2, 8, HALF, LEN), f32),
            pltpu.VMEM((SLOTS + 1, K, LEN), f32),
            pltpu.VMEM((2, 8, 2, 8, HALF, LEN), f32),
            pltpu.VMEM((2, 2, 2, 4, 8, HALF, LEN), f32),
            pltpu.VMEM((2, 2, 8, HALF, LEN), f32),
            pltpu.VMEM((2, 2, 8, HALF, LEN), f32),
            pltpu.VMEM((2, HALF, LEN), f32),
            pltpu.VMEM((2, HALF, LEN), f32),
            pltpu.VMEM((8, K, LEN), f32),
            pltpu.VMEM((8, K, LEN), f32),
            pltpu.VMEM((4, 16, LEN), f32),
            pltpu.VMEM((16, LEN), f32),
            pltpu.VMEM((3, 8, 16, LEN), f32),
            pltpu.VMEM((4, 8, LEN), f32),
            pltpu.VMEM((8, LEN), f32),
            pltpu.VMEM((3, 8, 8, LEN), f32),
            dma((8,)), dma(()),
            dma((8,)), dma((8,)),
            dma((2,)), dma((2,)),
            dma((2, 2, 8)), dma((2, 2, 8)),
            dma((2, 2, 2, 4)), dma((2, 2, 2, 4)),
            dma((2, 2, 2, 4)), dma((2, 2, 2, 4)),
            dma((2, 2, 8)), dma((2, 2, 8)),
            dma((2,)), dma((2,)),
            dma((8,)), dma((8,)),
            dma(()), dma(()),
            dma((3, 8)), dma((3, 8)),
            dma(()), dma(()),
            dma((3, 8)), dma((3, 8)),
        ],
        compiler_params=pltpu.CompilerParams(
            collective_id=0, has_side_effects=True, vmem_limit_bytes=VMEM_LIMIT
        ),
        name="exchange",
    )(
        tile_rows.reshape(SLOTS), tile_cols.reshape(SLOTS), counts, basis, previous, coupling,
        energies.reshape(1, LEN), tile_values.reshape(SLOTS, LEN, LEN),
    )
    return pl.pallas_call(
        deliver_kernel,
        out_shape=(
            jax.ShapeDtypeStruct((K, K), f32),
            jax.ShapeDtypeStruct((K, K), f32),
            jax.ShapeDtypeStruct((K, LEN), f32),
        ),
        in_specs=[vmem],
        out_specs=(vmem, vmem, vmem),
        compiler_params=pltpu.CompilerParams(vmem_limit_bytes=VMEM_LIMIT),
        name="deliver",
    )(out)


def solution(mesh):
    split_mesh = Mesh(mesh.devices.reshape(4, 2, 8, 8, 2), AXES)
    both = ROW + COL
    in_specs = (
        P(None, both),
        P(None, both),
        P(),
        P(both),
        P(ROW, COL, None, None, None),
        P(ROW, COL, None),
        P(ROW, COL, None),
        P(ROW, COL),
    )
    out_specs = (P(), P(), P(None, both))
    return jax.shard_map(
        shards, mesh=split_mesh, in_specs=in_specs, out_specs=out_specs, check_vma=False
    )
```

```python
import functools

import jax
import jax.numpy as jnp
from jax import lax
from jax.experimental import pallas as pl
from jax.experimental.pallas import tpu as pltpu
from jax.sharding import Mesh
from jax.sharding import PartitionSpec as P

AXES = ("zl", "co", "y", "x", "zh")
ROW = ("zl", "co")
COL = ("y", "x", "zh")
K = 32
HALF = 16
LEN = 128
SLOTS = 16
VMEM_LIMIT = 64 * 1024 * 1024 - 65536
RING = 8
MESH = pl.DeviceIdType.MESH
HIGHEST = lax.Precision.HIGHEST
NT = (((1,), (1,)), ((), ()))
NN = (((1,), (0,)), ((), ()))


def split(value):
    high = value.astype(jnp.bfloat16)
    low = (value - high.astype(jnp.float32)).astype(jnp.bfloat16)
    return high, low


def dot_three(left, right, dims):
    lh, ll = left
    rh, rl = right
    both = lax.dot_general(
        jnp.concatenate([lh, ll], axis=0), rh, dims, preferred_element_type=jnp.float32
    )
    rest = lax.dot_general(lh, rl, dims, preferred_element_type=jnp.float32)
    return both[:K] + (both[K:] + rest)


def exact_dot(left, right, dims):
    return lax.dot_general(
        left, right, dims, precision=HIGHEST, preferred_element_type=jnp.float32
    )


def remote(src, dst, send, recv, where):
    return pltpu.make_async_remote_copy(
        src_ref=src, dst_ref=dst, send_sem=send, recv_sem=recv, device_id=where, device_id_type=MESH
    )


def pack(block):
    out = block[:8]
    for q in range(1, 4):
        out = out + pltpu.roll(block[8 * q : 8 * q + 8], 32 * q, 1)
    return out


def unpack(block):
    return jnp.concatenate([block[:, 32 * q : 32 * q + 32] for q in range(4)], axis=0)


def wide(block):
    return jnp.concatenate([block, jnp.zeros((K, LEN - K), jnp.float32)], axis=1)


def finish(state_count, alpha_sum, basis_sum, image_sum, vectors, applied, alpha_out, beta_out, next_out):
    alpha = alpha_sum * (1.0 / state_count)
    basis_gram = basis_sum * (1.0 / state_count)
    alpha_t = alpha.T
    square = exact_dot(alpha_t, alpha, NN)
    projected = exact_dot(alpha_t, exact_dot(basis_gram, alpha, NN), NN)
    residual = applied - exact_dot(alpha_t, vectors, NN)
    alpha_out[...] = alpha
    gram = image_sum() * (1.0 / state_count) - 2.0 * square + projected
    upper, inverse = factor(gram)
    beta_out[...] = upper
    next_out[...] = exact_dot(inverse, residual, NN)


def factor(gram):
    at_row = lax.broadcasted_iota(jnp.int32, (K, K), 0)
    at_col = lax.broadcasted_iota(jnp.int32, (K, K), 1)
    work = jnp.concatenate([gram, jnp.where(at_row == at_col, 1.0, 0.0)], axis=1)
    done = []
    sub = lax.broadcasted_iota(jnp.int32, (8, 2 * K), 0)
    for q in range(4):
        block = work[:8]
        rest = work[8:]
        left = 24 - 8 * q
        heads = [jnp.broadcast_to(block[:, 8 * q + k : 8 * q + k + 1], (8, 2 * K)) for k in range(8)]
        rows = [jnp.broadcast_to(block[k : k + 1, :], (8, 2 * K)) for k in range(8)]
        full = {}
        for k in range(8):
            for m in range(k, 8):
                full[k, m] = jnp.broadcast_to(heads[m][k : k + 1, :], (8, 2 * K))
        if left:
            cols = [
                jnp.broadcast_to(rest[:, 8 * q + k : 8 * q + k + 1], (left, 2 * K)).reshape(left // 8, 8, 2 * K)
                for k in range(8)
            ]
            rest = rest.reshape(left // 8, 8, 2 * K)
        out = jnp.zeros((8, 2 * K), jnp.float32)
        for k in range(8):
            pivot = full[k, k]
            scale = 1.0 / pivot
            root = lax.rsqrt(pivot)
            root = root * (1.5 - 0.5 * pivot * root * root)
            out = jnp.where(sub == k, rows[k] * root, out)
            factors = {m: full[k, m] * scale for m in range(k + 1, 8)}
            for m in range(k + 1, 8):
                for n in range(m, 8):
                    full[m, n] = full[m, n] - full[k, n] * factors[m]
            for m in range(k + 1, 8):
                rows[m] = rows[m] - rows[k] * factors[m]
            if left:
                rest = rest - cols[k] * (rows[k] * scale)[None]
                for m in range(k + 1, 8):
                    cols[m] = cols[m] - cols[k] * factors[m][None]
        done.append(out)
        if left:
            work = rest.reshape(left, 2 * K)
    both = jnp.concatenate(done, axis=0)
    return jnp.where(at_row <= at_col, both[:, :K], 0.0), both[:, K:]


def exchange_kernel(
    state_count,
    rows_hbm, cols_hbm, count_hbm, basis_hbm, previous_hbm, coupling_hbm, energies_hbm, tiles_hbm,
    out,
    rows, cols, count, inv, inv_lanes, basis, previous, coupling, energies,
    tiles, cstates, rstates, direct, part, ring_in, last, last_in, mid, z_in, msum, m_in,
    early, early_in, early_dim, late, late_in, late_dim,
    in_sem, inv_sem,
    rg_s, rg_r, z0_s, z0_r, ex_s, ex_r, ag_s, ag_r, rs_s, rs_r, rx_s, rx_r, rz_s, rz_r, mr_s, mr_r,
    ec_s, ec_r, er_s, er_r, lc_s, lc_r, lr_s, lr_r,
):
    zl, co, y, x, zh = (lax.axis_index(a) for a in AXES)
    me_row = zl * 2 + co
    me_z = zh * 4 + zl
    zo = 1 - zh
    ring_pos = (y, x)
    exch_pos = (x, y)
    ring_axis = ("y", "x")
    exch_axis = ("x", "y")
    order = (4, 3, 5, 2, 6, 1, 7)

    def row_id(r):
        return {"zl": lax.div(r, 2), "co": lax.rem(r, 2)}

    def z_id(z):
        return {"zh": lax.div(z, 4), "zl": lax.rem(z, 4)}

    loads = [
        pltpu.make_async_copy(src, dst, in_sem.at[i])
        for i, (src, dst) in enumerate(
            (
                (basis_hbm, basis), (rows_hbm, rows), (count_hbm, count), (cols_hbm, cols), (tiles_hbm, tiles),
                (previous_hbm, previous), (coupling_hbm, coupling), (energies_hbm, energies),
            )
        )
    ]
    loads[0].start()
    barrier = pltpu.get_barrier_semaphore()

    def hello(where):
        pl.semaphore_signal(barrier, inc=1, device_id=where, device_id_type=MESH)

    for d in order:
        hello({"x": lax.rem(x + d, 8)})
        hello({"y": lax.rem(y + d, 8)})
        hello(row_id(lax.rem(me_row + d, 8)))
    for d in range(4):
        hello({"zh": zo, "zl": lax.rem(zl + d, 4)})

    for copy in loads[1:]:
        copy.start()
    direct[SLOTS] = jnp.zeros((K, LEN), jnp.float32)
    loads[0].wait()
    for h in range(2):
        rstates[h, ring_pos[h], zh, exch_pos[h]] = basis[h * HALF : (h + 1) * HALF, :]
    cstates[me_row] = basis[...]
    pl.semaphore_wait(barrier, 25)

    sends = []

    def go(copy):
        copy.start()
        sends.append(copy)

    for h in range(2):
        slot = rstates.at[h, ring_pos[h], zh, exch_pos[h]]
        go(remote(basis.at[pl.ds(h * HALF, HALF)], slot, z0_s.at[h], z0_r.at[h], {"zh": zo}))
    for d in order:
        for h in range(2):
            slot = rstates.at[h, ring_pos[h], zh, exch_pos[h]]
            go(
                remote(
                    basis.at[pl.ds(h * HALF, HALF)], slot, ex_s.at[h, 0, d], ex_r.at[h, 0, d],
                    {exch_axis[h]: lax.rem(exch_pos[h] + d, 8)},
                )
            )
        go(remote(basis, cstates.at[me_row], rg_s.at[d], rg_r.at[d], row_id(lax.rem(me_row + d, 8))))

    loads[1].wait()
    loads[2].wait()
    live = count[0, 0]
    lane = lax.broadcasted_iota(jnp.int32, (8, LEN), 1)
    table = jnp.full((8, LEN), SLOTS, jnp.int32)
    for s in range(SLOTS):
        table = jnp.where(lane == jnp.where(s < live, rows[s], -1), s, table)
    inv_lanes[...] = table
    inv_copy = pltpu.make_async_copy(inv_lanes.at[pl.ds(0, 1)], inv, inv_sem)
    inv_copy.start()

    def exch_wait(h, c):
        zc = (zh, zo)[c]
        for d in range(1, 8):
            slot = rstates.at[h, ring_pos[h], zc, lax.rem(exch_pos[h] + 8 - d, 8)]
            remote(slot, slot, ex_s.at[h, c, d], ex_r.at[h, c, d], {exch_axis[h]: exch_pos[h]}).wait_recv()

    def hops(sign, c):
        return 4 if (sign > 0) == (c == 0) else 3

    def ag_copy(h, g, c, s):
        sign = (1, -1)[g]
        zc = (zh, zo)[c]
        slot = rstates.at[h, lax.rem(ring_pos[h] + 8 - sign * (s - 1), 8), zc]
        return remote(
            slot, slot, ag_s.at[h, g, c, s - 1], ag_r.at[h, g, c, s - 1],
            {ring_axis[h]: lax.rem(ring_pos[h] + 8 + sign, 8)},
        )

    def ag_wait(h, g, c, s):
        sign = (1, -1)[g]
        zc = (zh, zo)[c]
        slot = rstates.at[h, lax.rem(ring_pos[h] + 8 - sign * s, 8), zc]
        remote(
            slot, slot, ag_s.at[h, g, c, s - 1], ag_r.at[h, g, c, s - 1],
            {ring_axis[h]: lax.rem(ring_pos[h] + 8 + sign, 8)},
        ).wait_recv()

    for h in range(2):
        slot = rstates.at[h, ring_pos[h], zo, exch_pos[h]]
        remote(slot, slot, z0_s.at[h], z0_r.at[h], {"zh": zo}).wait_recv()
        for d in order:
            go(
                remote(
                    slot, slot, ex_s.at[h, 1, d], ex_r.at[h, 1, d],
                    {exch_axis[h]: lax.rem(exch_pos[h] + d, 8)},
                )
            )
    for h in range(2):
        exch_wait(h, 0)
        for g in range(2):
            go(ag_copy(h, g, 0, 1))

    for d in range(1, 8):
        slot = cstates.at[lax.rem(me_row + 8 - d, 8)]
        remote(slot, slot, rg_s.at[d], rg_r.at[d], row_id(me_row)).wait_recv()
    for copy in loads[3:]:
        copy.wait()
    inv_copy.wait()
    for s in range(SLOTS):
        direct[s] = dot_three(split(cstates[cols[s]]), split(tiles[s]), NT)

    for a in range(8):
        for b in range(8):
            for z in range(2):
                value = direct[inv[0, (a * 8 + b) * 2 + z]]
                part[0, a, z, b] = value[:HALF]
                part[1, b, z, a] = value[HALF:]

    def rs_copy(h, g, c, s):
        sign = (1, -1)[g]
        zc = (zo, zh)[c]
        slot = part.at[h, lax.rem(ring_pos[h] + 8 + sign * (5 - s), 8), zc]
        return remote(
            slot, ring_in.at[h, g, c, s - 1], rs_s.at[h, g, c, s - 1], rs_r.at[h, g, c, s - 1],
            {ring_axis[h]: lax.rem(ring_pos[h] + 8 + sign, 8)},
        )

    def rs_wait(h, g, c, s):
        slot = ring_in.at[h, g, c, s - 1]
        sign = (1, -1)[g]
        remote(
            slot, slot, rs_s.at[h, g, c, s - 1], rs_r.at[h, g, c, s - 1],
            {ring_axis[h]: lax.rem(ring_pos[h] + 8 + sign, 8)},
        ).wait_recv()

    def rs_step(c, s):
        zc = (zo, zh)[c]
        for h in range(2):
            for g in range(2):
                sign = (1, -1)[g]
                n = hops(sign, c)
                if s == 0:
                    if n == 4:
                        go(rs_copy(h, g, c, 1))
                    continue
                if n == 4 or s > 1:
                    rs_wait(h, g, c, s)
                if s < 4:
                    to = lax.rem(ring_pos[h] + 8 + sign * (4 - s), 8)
                    if n == 4 or s > 1:
                        part[h, to, zc] = part[h, to, zc] + ring_in[h, g, c, s - 1]
                    go(rs_copy(h, g, c, s + 1))

    def rs_last(c):
        zc = (zo, zh)[c]
        for h in range(2):
            last[h, c] = part[h, ring_pos[h], zc] + (ring_in[h, 0, c, 3] + ring_in[h, 1, c, 3])
            for d in order:
                to = lax.rem(exch_pos[h] + d, 8)
                go(
                    remote(
                        last.at[h, c, to], last_in.at[h, c, d], rx_s.at[h, c, d], rx_r.at[h, c, d],
                        {exch_axis[h]: to},
                    )
                )

    def ag_flow(c, s):
        for h in range(2):
            for g in range(2):
                n = hops((1, -1)[g], c)
                if s <= n:
                    ag_wait(h, g, c, s)
                    if s < n:
                        go(ag_copy(h, g, c, s + 1))

    mirror = []
    row_parts = []

    def mirror_step(tiles_from, tiles_to):
        for s in range(tiles_from, tiles_to):
            t = rows[s]
            at_y, at_x, at_z = lax.div(t, 16), lax.rem(lax.div(t, 2), 8), lax.rem(t, 2)
            picked = split(
                jnp.concatenate([rstates[0, at_y, at_z, at_x], rstates[1, at_x, at_z, at_y]], axis=0)
            )
            row_parts.append(picked)
            mirror.append(dot_three(picked, split(tiles[s]), NN))

    def drain():
        while sends:
            sends.pop(0).wait_send()

    rs_step(0, 0)
    ag_flow(0, 1)
    rs_step(1, 0)
    for h in range(2):
        exch_wait(h, 1)
        for g in range(2):
            go(ag_copy(h, g, 1, 1))
    rs_step(0, 1)
    ag_flow(1, 1)
    for s in range(2, 5):
        ag_flow(0, s)
        rs_step(0, s)
        if s == 4:
            rs_last(0)
        rs_step(1, s - 1)
        ag_flow(1, s)
    mirror_step(0, SLOTS)
    weights = [[jnp.where((cols[s] == u) & (s < live), 1.0, 0.0) for s in range(SLOTS)] for u in range(8)]
    for u in range(8):
        total = weights[u][0] * mirror[0]
        for s in range(1, SLOTS):
            total = total + weights[u][s] * mirror[s]
        msum[u] = total
    for d in order:
        to = lax.rem(me_row + d, 8)
        go(remote(msum.at[to], m_in.at[d], mr_s.at[d], mr_r.at[d], row_id(to)))

    def core_start(src, dst, send, recv):
        go(remote(src, dst, send, recv, {"co": 1 - co}))

    def core_wait(dst, send, recv):
        remote(dst, dst, send, recv, {"co": 1 - co}).wait_recv()

    def dim_start(dim, src, dst, send, recv):
        for d in order:
            where = ({"x": lax.rem(x + d, 8)}, {"y": lax.rem(y + d, 8)}, z_id(lax.rem(me_z + d, 8)))[dim]
            go(remote(src, dst.at[dim, d], send.at[dim, d], recv.at[dim, d], where))

    def dim_wait(dim, mine, dst, send, recv):
        for d in range(1, 8):
            slot = dst.at[dim, d]
            remote(slot, slot, send.at[dim, d], recv.at[dim, d], {"x": x}).wait_recv()
        dst[dim, 0] = mine
        here = (x, y, me_z)[dim]
        total = dst[dim, here]
        for k in range(1, 8):
            total = total + dst[dim, lax.rem(here + 8 - k, 8)]
        return total

    vectors = basis[...]
    own = energies[...] * vectors - exact_dot(coupling[...], previous[...], NN)
    live_direct = [split(jnp.where(s < live, 1.0, 0.0) * direct[s]) for s in range(SLOTS)]
    rh = jnp.concatenate([p[0] for p in row_parts], axis=1)
    rl = jnp.concatenate([p[1] for p in row_parts], axis=1)
    dh = jnp.concatenate([p[0] for p in live_direct], axis=1)
    dl = jnp.concatenate([p[1] for p in live_direct], axis=1)
    cross = lax.dot_general(jnp.concatenate([rh, rl], axis=0), dh, NT, preferred_element_type=jnp.float32)
    cross = cross[:K] + (cross[K:] + lax.dot_general(rh, dl, NT, preferred_element_type=jnp.float32))
    cross = cross + cross.T + exact_dot(vectors, own, NT)
    early[0, :8] = pack(wide(cross))
    early[0, 8:] = pack(wide(exact_dot(vectors, vectors, NT)))
    core_start(early.at[0], early_in, ec_s, ec_r)
    rs_step(1, 4)
    rs_last(1)

    def last_sum(c, h):
        total = last[h, c, exch_pos[h]]
        for d in range(1, 8):
            slot = last_in.at[h, c, d]
            remote(slot, slot, rx_s.at[h, c, d], rx_r.at[h, c, d], {exch_axis[h]: exch_pos[h]}).wait_recv()
            total = total + last_in[h, c, d]
        return total

    for h in range(2):
        mid[h] = last_sum(0, h)
        go(remote(mid.at[h], z_in.at[h], rz_s.at[h], rz_r.at[h], {"zh": zo}))

    core_wait(early_in, ec_s, ec_r)
    early[1] = early[0] + early_in[...]
    dim_start(0, early.at[1], early_dim, er_s, er_r)
    halves = [last_sum(1, h) for h in range(2)]
    for d in range(1, 8):
        slot = m_in.at[d]
        remote(slot, slot, mr_s.at[d], mr_r.at[d], row_id(me_row)).wait_recv()
    applied = own + msum[me_row]
    for d in range(1, 8):
        applied = applied + m_in[d]
    for h in range(2):
        slot = z_in.at[h]
        remote(slot, slot, rz_s.at[h], rz_r.at[h], {"zh": zo}).wait_recv()
    applied = applied + jnp.concatenate([halves[0] + z_in[0], halves[1] + z_in[1]], axis=0)

    late[0] = pack(wide(exact_dot(applied, applied, NT)))
    core_start(late.at[0], late_in, lc_s, lc_r)
    core_wait(late_in, lc_s, lc_r)
    late[1] = late[0] + late_in[...]
    dim_start(0, late.at[1], late_dim, lr_s, lr_r)
    early[2] = dim_wait(0, early[1], early_dim, er_s, er_r)
    dim_start(1, early.at[2], early_dim, er_s, er_r)
    late[2] = dim_wait(0, late[1], late_dim, lr_s, lr_r)
    dim_start(1, late.at[2], late_dim, lr_s, lr_r)
    early[3] = dim_wait(1, early[2], early_dim, er_s, er_r)
    dim_start(2, early.at[3], early_dim, er_s, er_r)
    drain()
    late[3] = dim_wait(1, late[2], late_dim, lr_s, lr_r)
    dim_start(2, late.at[3], late_dim, lr_s, lr_r)
    sums = dim_wait(2, early[3], early_dim, er_s, er_r)
    finish(
        state_count, unpack(sums[:8]), unpack(sums[8:]),
        lambda: unpack(dim_wait(2, late[3], late_dim, lr_s, lr_r)),
        vectors, applied, out.at[pl.ds(K, K), pl.ds(0, K)], out.at[pl.ds(2 * K, K), pl.ds(0, K)], out.at[pl.ds(0, K)],
    )
    drain()


def deliver_kernel(packed, alpha_out, beta_out, next_out):
    next_out[...] = packed[:K, :]
    alpha_out[...] = packed[K : 2 * K, :K]
    beta_out[...] = packed[2 * K :, :K]


def shards(basis, previous, coupling, energies, tile_values, tile_rows, tile_cols, counts):
    state_count = basis.shape[1] * lax.axis_size(ROW) * lax.axis_size(COL)
    f32, i32 = jnp.float32, jnp.int32
    vmem = pl.BlockSpec(memory_space=pltpu.VMEM)
    dma = pltpu.SemaphoreType.DMA
    out = pl.pallas_call(
        functools.partial(exchange_kernel, state_count),
        out_shape=jax.ShapeDtypeStruct((3 * K, LEN), f32),
        in_specs=[pl.BlockSpec(memory_space=pl.ANY)] * 8,
        out_specs=vmem,
        scratch_shapes=[
            pltpu.SMEM((SLOTS,), i32),
            pltpu.SMEM((SLOTS,), i32),
            pltpu.SMEM((1, 1), i32),
            pltpu.SMEM((1, LEN), i32),
            pltpu.VMEM((8, LEN), i32),
            pltpu.VMEM((K, LEN), f32),
            pltpu.VMEM((K, LEN), f32),
            pltpu.VMEM((K, K), f32),
            pltpu.VMEM((1, LEN), f32),
            pltpu.VMEM((SLOTS, LEN, LEN), f32),
            pltpu.VMEM((8, K, LEN), f32),
            pltpu.VMEM((2, 8, 2, 8, HALF, LEN), f32),
            pltpu.VMEM((SLOTS + 1, K, LEN), f32),
            pltpu.VMEM((2, 8, 2, 8, HALF, LEN), f32),
            pltpu.VMEM((2, 2, 2, 4, 8, HALF, LEN), f32),
            pltpu.VMEM((2, 2, 8, HALF, LEN), f32),
            pltpu.VMEM((2, 2, 8, HALF, LEN), f32),
            pltpu.VMEM((2, HALF, LEN), f32),
            pltpu.VMEM((2, HALF, LEN), f32),
            pltpu.VMEM((8, K, LEN), f32),
            pltpu.VMEM((8, K, LEN), f32),
            pltpu.VMEM((4, 16, LEN), f32),
            pltpu.VMEM((16, LEN), f32),
            pltpu.VMEM((3, 8, 16, LEN), f32),
            pltpu.VMEM((4, 8, LEN), f32),
            pltpu.VMEM((8, LEN), f32),
            pltpu.VMEM((3, 8, 8, LEN), f32),
            dma((8,)), dma(()),
            dma((8,)), dma((8,)),
            dma((2,)), dma((2,)),
            dma((2, 2, 8)), dma((2, 2, 8)),
            dma((2, 2, 2, 4)), dma((2, 2, 2, 4)),
            dma((2, 2, 2, 4)), dma((2, 2, 2, 4)),
            dma((2, 2, 8)), dma((2, 2, 8)),
            dma((2,)), dma((2,)),
            dma((8,)), dma((8,)),
            dma(()), dma(()),
            dma((3, 8)), dma((3, 8)),
            dma(()), dma(()),
            dma((3, 8)), dma((3, 8)),
        ],
        compiler_params=pltpu.CompilerParams(
            collective_id=0, has_side_effects=True, vmem_limit_bytes=VMEM_LIMIT
        ),
        name="exchange",
    )(
        tile_rows.reshape(SLOTS), tile_cols.reshape(SLOTS), counts, basis, previous, coupling,
        energies.reshape(1, LEN), tile_values.reshape(SLOTS, LEN, LEN),
    )
    return pl.pallas_call(
        deliver_kernel,
        out_shape=(
            jax.ShapeDtypeStruct((K, K), f32),
            jax.ShapeDtypeStruct((K, K), f32),
            jax.ShapeDtypeStruct((K, LEN), f32),
        ),
        in_specs=[vmem],
        out_specs=(vmem, vmem, vmem),
        compiler_params=pltpu.CompilerParams(vmem_limit_bytes=VMEM_LIMIT),
        name="deliver",
    )(out)


def solution(mesh):
    split_mesh = Mesh(mesh.devices.reshape(4, 2, 8, 8, 2), AXES)
    both = ROW + COL
    in_specs = (
        P(None, both),
        P(None, both),
        P(),
        P(both),
        P(ROW, COL, None, None, None),
        P(ROW, COL, None),
        P(ROW, COL, None),
        P(ROW, COL),
    )
    out_specs = (P(), P(), P(None, both))
    return jax.shard_map(
        shards, mesh=split_mesh, in_specs=in_specs, out_specs=out_specs, check_vma=False
    )
```

```python
import functools

import jax
import jax.numpy as jnp
from jax import lax
from jax.experimental import pallas as pl
from jax.experimental.pallas import tpu as pltpu
from jax.sharding import Mesh
from jax.sharding import PartitionSpec as P

AXES = ("zl", "co", "y", "x", "zh")
ROW = ("zl", "co")
COL = ("y", "x", "zh")
K = 32
HALF = 16
LEN = 128
SLOTS = 16
VMEM_LIMIT = 64 * 1024 * 1024 - 65536
RING = 8
MESH = pl.DeviceIdType.MESH
HIGHEST = lax.Precision.HIGHEST
NT = (((1,), (1,)), ((), ()))
NN = (((1,), (0,)), ((), ()))


def split(value):
    high = value.astype(jnp.bfloat16)
    low = (value - high.astype(jnp.float32)).astype(jnp.bfloat16)
    return high, low


def dot_three(left, right, dims):
    lh, ll = left
    rh, rl = right
    both = lax.dot_general(
        jnp.concatenate([lh, ll], axis=0), rh, dims, preferred_element_type=jnp.float32
    )
    rest = lax.dot_general(lh, rl, dims, preferred_element_type=jnp.float32)
    return both[:K] + (both[K:] + rest)


def exact_dot(left, right, dims):
    return lax.dot_general(
        left, right, dims, precision=HIGHEST, preferred_element_type=jnp.float32
    )


def remote(src, dst, send, recv, where):
    return pltpu.make_async_remote_copy(
        src_ref=src, dst_ref=dst, send_sem=send, recv_sem=recv, device_id=where, device_id_type=MESH
    )


def pack(block):
    out = block[:8]
    for q in range(1, 4):
        out = out + pltpu.roll(block[8 * q : 8 * q + 8], 32 * q, 1)
    return out


def unpack(block):
    return jnp.concatenate([block[:, 32 * q : 32 * q + 32] for q in range(4)], axis=0)


def wide(block):
    return jnp.concatenate([block, jnp.zeros((K, LEN - K), jnp.float32)], axis=1)


def finish(state_count, alpha_sum, basis_sum, image_sum, vectors, applied, alpha_out, beta_out, next_out):
    alpha = alpha_sum * (1.0 / state_count)
    basis_gram = basis_sum * (1.0 / state_count)
    alpha_t = alpha.T
    square = exact_dot(alpha_t, alpha, NN)
    projected = exact_dot(alpha_t, exact_dot(basis_gram, alpha, NN), NN)
    residual = applied - exact_dot(alpha_t, vectors, NN)
    alpha_out[...] = alpha
    gram = image_sum() * (1.0 / state_count) - 2.0 * square + projected
    upper, inverse = factor(gram)
    beta_out[...] = upper
    next_out[...] = exact_dot(inverse, residual, NN)


def factor(gram):
    at_row = lax.broadcasted_iota(jnp.int32, (K, K), 0)
    at_col = lax.broadcasted_iota(jnp.int32, (K, K), 1)
    work = jnp.concatenate([gram, jnp.where(at_row == at_col, 1.0, 0.0)], axis=1)
    done = []
    sub = lax.broadcasted_iota(jnp.int32, (8, 2 * K), 0)
    for q in range(4):
        block = work[:8]
        rest = work[8:]
        left = 24 - 8 * q
        heads = [jnp.broadcast_to(block[:, 8 * q + k : 8 * q + k + 1], (8, 2 * K)) for k in range(8)]
        rows = [jnp.broadcast_to(block[k : k + 1, :], (8, 2 * K)) for k in range(8)]
        full = {}
        for k in range(8):
            for m in range(k, 8):
                full[k, m] = jnp.broadcast_to(heads[m][k : k + 1, :], (8, 2 * K))
        if left:
            cols = [
                jnp.broadcast_to(rest[:, 8 * q + k : 8 * q + k + 1], (left, 2 * K)).reshape(left // 8, 8, 2 * K)
                for k in range(8)
            ]
            rest = rest.reshape(left // 8, 8, 2 * K)
        out = jnp.zeros((8, 2 * K), jnp.float32)
        for k in range(8):
            pivot = full[k, k]
            scale = 1.0 / pivot
            root = lax.rsqrt(pivot)
            root = root * (1.5 - 0.5 * pivot * root * root)
            out = jnp.where(sub == k, rows[k] * root, out)
            factors = {m: full[k, m] * scale for m in range(k + 1, 8)}
            for m in range(k + 1, 8):
                for n in range(m, 8):
                    full[m, n] = full[m, n] - full[k, n] * factors[m]
            for m in range(k + 1, 8):
                rows[m] = rows[m] - rows[k] * factors[m]
            if left:
                rest = rest - cols[k] * (rows[k] * scale)[None]
                for m in range(k + 1, 8):
                    cols[m] = cols[m] - cols[k] * factors[m][None]
        done.append(out)
        if left:
            work = rest.reshape(left, 2 * K)
    both = jnp.concatenate(done, axis=0)
    return jnp.where(at_row <= at_col, both[:, :K], 0.0), both[:, K:]


def exchange_kernel(
    state_count,
    rows_hbm, cols_hbm, count_hbm, basis_hbm, previous_hbm, coupling_hbm, energies_hbm, tiles_hbm,
    out,
    rows, cols, count, inv, inv_lanes, basis, previous, coupling, energies,
    tiles, cstates, rstates, direct, part, ring_in, last, last_in, mid, z_in, msum, m_in,
    early, early_in, early_dim, late, late_in, late_dim,
    in_sem, inv_sem,
    rg_s, rg_r, z0_s, z0_r, ex_s, ex_r, ag_s, ag_r, rs_s, rs_r, rx_s, rx_r, rz_s, rz_r, mr_s, mr_r,
    ec_s, ec_r, er_s, er_r, lc_s, lc_r, lr_s, lr_r,
):
    zl, co, y, x, zh = (lax.axis_index(a) for a in AXES)
    me_row = zl * 2 + co
    me_z = zh * 4 + zl
    zo = 1 - zh
    ring_pos = (y, x)
    exch_pos = (x, y)
    ring_axis = ("y", "x")
    exch_axis = ("x", "y")
    order = (4, 3, 5, 2, 6, 1, 7)

    def row_id(r):
        return {"zl": lax.div(r, 2), "co": lax.rem(r, 2)}

    def z_id(z):
        return {"zh": lax.div(z, 4), "zl": lax.rem(z, 4)}

    loads = [
        pltpu.make_async_copy(src, dst, in_sem.at[i])
        for i, (src, dst) in enumerate(
            (
                (basis_hbm, basis), (rows_hbm, rows), (count_hbm, count), (cols_hbm, cols), (tiles_hbm, tiles),
                (previous_hbm, previous), (coupling_hbm, coupling), (energies_hbm, energies),
            )
        )
    ]
    loads[0].start()
    barrier = pltpu.get_barrier_semaphore()

    def hello(where):
        pl.semaphore_signal(barrier, inc=1, device_id=where, device_id_type=MESH)

    for d in order:
        hello({"x": lax.rem(x + d, 8)})
        hello({"y": lax.rem(y + d, 8)})
        hello(row_id(lax.rem(me_row + d, 8)))
    for d in range(4):
        hello({"zh": zo, "zl": lax.rem(zl + d, 4)})

    for copy in loads[1:]:
        copy.start()
    direct[SLOTS] = jnp.zeros((K, LEN), jnp.float32)
    loads[0].wait()
    for h in range(2):
        rstates[h, ring_pos[h], zh, exch_pos[h]] = basis[h * HALF : (h + 1) * HALF, :]
    cstates[me_row] = basis[...]
    pl.semaphore_wait(barrier, 25)

    sends = []

    def go(copy):
        copy.start()
        sends.append(copy)

    for h in range(2):
        slot = rstates.at[h, ring_pos[h], zh, exch_pos[h]]
        go(remote(basis.at[pl.ds(h * HALF, HALF)], slot, z0_s.at[h], z0_r.at[h], {"zh": zo}))
    for d in order:
        for h in range(2):
            slot = rstates.at[h, ring_pos[h], zh, exch_pos[h]]
            go(
                remote(
                    basis.at[pl.ds(h * HALF, HALF)], slot, ex_s.at[h, 0, d], ex_r.at[h, 0, d],
                    {exch_axis[h]: lax.rem(exch_pos[h] + d, 8)},
                )
            )
        go(remote(basis, cstates.at[me_row], rg_s.at[d], rg_r.at[d], row_id(lax.rem(me_row + d, 8))))

    loads[1].wait()
    loads[2].wait()
    live = count[0, 0]
    lane = lax.broadcasted_iota(jnp.int32, (8, LEN), 1)
    table = jnp.full((8, LEN), SLOTS, jnp.int32)
    for s in range(SLOTS):
        table = jnp.where(lane == jnp.where(s < live, rows[s], -1), s, table)
    inv_lanes[...] = table
    inv_copy = pltpu.make_async_copy(inv_lanes.at[pl.ds(0, 1)], inv, inv_sem)
    inv_copy.start()
    vectors = basis[...]
    for copy in loads[3:]:
        copy.wait()
    own = energies[...] * vectors - exact_dot(coupling[...], previous[...], NN)
    early[0, 8:] = pack(wide(exact_dot(vectors, vectors, NT)))
    own_cross = exact_dot(vectors, own, NT)

    def exch_wait(h, c):
        zc = (zh, zo)[c]
        for d in range(1, 8):
            slot = rstates.at[h, ring_pos[h], zc, lax.rem(exch_pos[h] + 8 - d, 8)]
            remote(slot, slot, ex_s.at[h, c, d], ex_r.at[h, c, d], {exch_axis[h]: exch_pos[h]}).wait_recv()

    def hops(sign, c):
        return 4 if (sign > 0) == (c == 0) else 3

    def ag_copy(h, g, c, s):
        sign = (1, -1)[g]
        zc = (zh, zo)[c]
        slot = rstates.at[h, lax.rem(ring_pos[h] + 8 - sign * (s - 1), 8), zc]
        return remote(
            slot, slot, ag_s.at[h, g, c, s - 1], ag_r.at[h, g, c, s - 1],
            {ring_axis[h]: lax.rem(ring_pos[h] + 8 + sign, 8)},
        )

    def ag_wait(h, g, c, s):
        sign = (1, -1)[g]
        zc = (zh, zo)[c]
        slot = rstates.at[h, lax.rem(ring_pos[h] + 8 - sign * s, 8), zc]
        remote(
            slot, slot, ag_s.at[h, g, c, s - 1], ag_r.at[h, g, c, s - 1],
            {ring_axis[h]: lax.rem(ring_pos[h] + 8 + sign, 8)},
        ).wait_recv()

    for h in range(2):
        slot = rstates.at[h, ring_pos[h], zo, exch_pos[h]]
        remote(slot, slot, z0_s.at[h], z0_r.at[h], {"zh": zo}).wait_recv()
        for d in order:
            go(
                remote(
                    slot, slot, ex_s.at[h, 1, d], ex_r.at[h, 1, d],
                    {exch_axis[h]: lax.rem(exch_pos[h] + d, 8)},
                )
            )
    for h in range(2):
        exch_wait(h, 0)
        for g in range(2):
            go(ag_copy(h, g, 0, 1))

    for d in range(1, 8):
        slot = cstates.at[lax.rem(me_row + 8 - d, 8)]
        remote(slot, slot, rg_s.at[d], rg_r.at[d], row_id(me_row)).wait_recv()
    inv_copy.wait()
    for s in range(SLOTS):
        direct[s] = dot_three(split(cstates[cols[s]]), split(tiles[s]), NT)

    for a in range(8):
        for b in range(8):
            for z in range(2):
                value = direct[inv[0, (a * 8 + b) * 2 + z]]
                part[0, a, z, b] = value[:HALF]
                part[1, b, z, a] = value[HALF:]

    def rs_copy(h, g, c, s):
        sign = (1, -1)[g]
        zc = (zo, zh)[c]
        slot = part.at[h, lax.rem(ring_pos[h] + 8 + sign * (5 - s), 8), zc]
        return remote(
            slot, ring_in.at[h, g, c, s - 1], rs_s.at[h, g, c, s - 1], rs_r.at[h, g, c, s - 1],
            {ring_axis[h]: lax.rem(ring_pos[h] + 8 + sign, 8)},
        )

    def rs_wait(h, g, c, s):
        slot = ring_in.at[h, g, c, s - 1]
        sign = (1, -1)[g]
        remote(
            slot, slot, rs_s.at[h, g, c, s - 1], rs_r.at[h, g, c, s - 1],
            {ring_axis[h]: lax.rem(ring_pos[h] + 8 + sign, 8)},
        ).wait_recv()

    def rs_step(c, s):
        zc = (zo, zh)[c]
        for h in range(2):
            for g in range(2):
                sign = (1, -1)[g]
                n = hops(sign, c)
                if s == 0:
                    if n == 4:
                        go(rs_copy(h, g, c, 1))
                    continue
                if n == 4 or s > 1:
                    rs_wait(h, g, c, s)
                if s < 4:
                    to = lax.rem(ring_pos[h] + 8 + sign * (4 - s), 8)
                    if n == 4 or s > 1:
                        part[h, to, zc] = part[h, to, zc] + ring_in[h, g, c, s - 1]
                    go(rs_copy(h, g, c, s + 1))

    def rs_last(c):
        zc = (zo, zh)[c]
        for h in range(2):
            last[h, c] = part[h, ring_pos[h], zc] + (ring_in[h, 0, c, 3] + ring_in[h, 1, c, 3])
            for d in order:
                to = lax.rem(exch_pos[h] + d, 8)
                go(
                    remote(
                        last.at[h, c, to], last_in.at[h, c, d], rx_s.at[h, c, d], rx_r.at[h, c, d],
                        {exch_axis[h]: to},
                    )
                )

    def ag_flow(c, s):
        for h in range(2):
            for g in range(2):
                n = hops((1, -1)[g], c)
                if s <= n:
                    ag_wait(h, g, c, s)
                    if s < n:
                        go(ag_copy(h, g, c, s + 1))

    mirror = []
    row_parts = []

    def mirror_step(tiles_from, tiles_to):
        for s in range(tiles_from, tiles_to):
            t = rows[s]
            at_y, at_x, at_z = lax.div(t, 16), lax.rem(lax.div(t, 2), 8), lax.rem(t, 2)
            picked = split(
                jnp.concatenate([rstates[0, at_y, at_z, at_x], rstates[1, at_x, at_z, at_y]], axis=0)
            )
            row_parts.append(picked)
            mirror.append(dot_three(picked, split(tiles[s]), NN))

    def drain():
        while sends:
            sends.pop(0).wait_send()

    rs_step(0, 0)
    ag_flow(0, 1)
    rs_step(1, 0)
    for h in range(2):
        exch_wait(h, 1)
        for g in range(2):
            go(ag_copy(h, g, 1, 1))
    rs_step(0, 1)
    ag_flow(1, 1)
    for s in range(2, 5):
        ag_flow(0, s)
        rs_step(0, s)
        if s == 4:
            rs_last(0)
        rs_step(1, s - 1)
        ag_flow(1, s)
    mirror_step(0, SLOTS)
    weights = [[jnp.where((cols[s] == u) & (s < live), 1.0, 0.0) for s in range(SLOTS)] for u in range(8)]
    for u in range(8):
        total = weights[u][0] * mirror[0]
        for s in range(1, SLOTS):
            total = total + weights[u][s] * mirror[s]
        msum[u] = total
    for d in order:
        to = lax.rem(me_row + d, 8)
        go(remote(msum.at[to], m_in.at[d], mr_s.at[d], mr_r.at[d], row_id(to)))

    def core_start(src, dst, send, recv):
        go(remote(src, dst, send, recv, {"co": 1 - co}))

    def core_wait(dst, send, recv):
        remote(dst, dst, send, recv, {"co": 1 - co}).wait_recv()

    def dim_start(dim, src, dst, send, recv):
        for d in order:
            where = ({"x": lax.rem(x + d, 8)}, {"y": lax.rem(y + d, 8)}, z_id(lax.rem(me_z + d, 8)))[dim]
            go(remote(src, dst.at[dim, d], send.at[dim, d], recv.at[dim, d], where))

    def dim_wait(dim, mine, dst, send, recv):
        for d in range(1, 8):
            slot = dst.at[dim, d]
            remote(slot, slot, send.at[dim, d], recv.at[dim, d], {"x": x}).wait_recv()
        dst[dim, 0] = mine
        here = (x, y, me_z)[dim]
        total = dst[dim, here]
        for k in range(1, 8):
            total = total + dst[dim, lax.rem(here + 8 - k, 8)]
        return total

    live_direct = [split(jnp.where(s < live, 1.0, 0.0) * direct[s]) for s in range(SLOTS)]
    rh = jnp.concatenate([p[0] for p in row_parts], axis=1)
    rl = jnp.concatenate([p[1] for p in row_parts], axis=1)
    dh = jnp.concatenate([p[0] for p in live_direct], axis=1)
    dl = jnp.concatenate([p[1] for p in live_direct], axis=1)
    cross = lax.dot_general(jnp.concatenate([rh, rl], axis=0), dh, NT, preferred_element_type=jnp.float32)
    cross = cross[:K] + (cross[K:] + lax.dot_general(rh, dl, NT, preferred_element_type=jnp.float32))
    cross = cross + cross.T + own_cross
    early[0, :8] = pack(wide(cross))
    core_start(early.at[0], early_in, ec_s, ec_r)
    rs_step(1, 4)
    rs_last(1)

    def last_sum(c, h):
        total = last[h, c, exch_pos[h]]
        for d in range(1, 8):
            slot = last_in.at[h, c, d]
            remote(slot, slot, rx_s.at[h, c, d], rx_r.at[h, c, d], {exch_axis[h]: exch_pos[h]}).wait_recv()
            total = total + last_in[h, c, d]
        return total

    for h in range(2):
        mid[h] = last_sum(0, h)
        go(remote(mid.at[h], z_in.at[h], rz_s.at[h], rz_r.at[h], {"zh": zo}))

    core_wait(early_in, ec_s, ec_r)
    early[1] = early[0] + early_in[...]
    dim_start(0, early.at[1], early_dim, er_s, er_r)
    halves = [last_sum(1, h) for h in range(2)]
    for d in range(1, 8):
        slot = m_in.at[d]
        remote(slot, slot, mr_s.at[d], mr_r.at[d], row_id(me_row)).wait_recv()
    applied = own + msum[me_row]
    for d in range(1, 8):
        applied = applied + m_in[d]
    for h in range(2):
        slot = z_in.at[h]
        remote(slot, slot, rz_s.at[h], rz_r.at[h], {"zh": zo}).wait_recv()
    applied = applied + jnp.concatenate([halves[0] + z_in[0], halves[1] + z_in[1]], axis=0)

    late[0] = pack(wide(exact_dot(applied, applied, NT)))
    core_start(late.at[0], late_in, lc_s, lc_r)
    core_wait(late_in, lc_s, lc_r)
    late[1] = late[0] + late_in[...]
    dim_start(0, late.at[1], late_dim, lr_s, lr_r)
    early[2] = dim_wait(0, early[1], early_dim, er_s, er_r)
    dim_start(1, early.at[2], early_dim, er_s, er_r)
    late[2] = dim_wait(0, late[1], late_dim, lr_s, lr_r)
    dim_start(1, late.at[2], late_dim, lr_s, lr_r)
    early[3] = dim_wait(1, early[2], early_dim, er_s, er_r)
    dim_start(2, early.at[3], early_dim, er_s, er_r)
    drain()
    late[3] = dim_wait(1, late[2], late_dim, lr_s, lr_r)
    dim_start(2, late.at[3], late_dim, lr_s, lr_r)
    sums = dim_wait(2, early[3], early_dim, er_s, er_r)
    finish(
        state_count, unpack(sums[:8]), unpack(sums[8:]),
        lambda: unpack(dim_wait(2, late[3], late_dim, lr_s, lr_r)),
        vectors, applied, out.at[pl.ds(K, K), pl.ds(0, K)], out.at[pl.ds(2 * K, K), pl.ds(0, K)], out.at[pl.ds(0, K)],
    )
    drain()


def deliver_kernel(packed, alpha_out, beta_out, next_out):
    next_out[...] = packed[:K, :]
    alpha_out[...] = packed[K : 2 * K, :K]
    beta_out[...] = packed[2 * K :, :K]


def shards(basis, previous, coupling, energies, tile_values, tile_rows, tile_cols, counts):
    state_count = basis.shape[1] * lax.axis_size(ROW) * lax.axis_size(COL)
    f32, i32 = jnp.float32, jnp.int32
    vmem = pl.BlockSpec(memory_space=pltpu.VMEM)
    dma = pltpu.SemaphoreType.DMA
    out = pl.pallas_call(
        functools.partial(exchange_kernel, state_count),
        out_shape=jax.ShapeDtypeStruct((3 * K, LEN), f32),
        in_specs=[pl.BlockSpec(memory_space=pl.ANY)] * 8,
        out_specs=vmem,
        scratch_shapes=[
            pltpu.SMEM((SLOTS,), i32),
            pltpu.SMEM((SLOTS,), i32),
            pltpu.SMEM((1, 1), i32),
            pltpu.SMEM((1, LEN), i32),
            pltpu.VMEM((8, LEN), i32),
            pltpu.VMEM((K, LEN), f32),
            pltpu.VMEM((K, LEN), f32),
            pltpu.VMEM((K, K), f32),
            pltpu.VMEM((1, LEN), f32),
            pltpu.VMEM((SLOTS, LEN, LEN), f32),
            pltpu.VMEM((8, K, LEN), f32),
            pltpu.VMEM((2, 8, 2, 8, HALF, LEN), f32),
            pltpu.VMEM((SLOTS + 1, K, LEN), f32),
            pltpu.VMEM((2, 8, 2, 8, HALF, LEN), f32),
            pltpu.VMEM((2, 2, 2, 4, 8, HALF, LEN), f32),
            pltpu.VMEM((2, 2, 8, HALF, LEN), f32),
            pltpu.VMEM((2, 2, 8, HALF, LEN), f32),
            pltpu.VMEM((2, HALF, LEN), f32),
            pltpu.VMEM((2, HALF, LEN), f32),
            pltpu.VMEM((8, K, LEN), f32),
            pltpu.VMEM((8, K, LEN), f32),
            pltpu.VMEM((4, 16, LEN), f32),
            pltpu.VMEM((16, LEN), f32),
            pltpu.VMEM((3, 8, 16, LEN), f32),
            pltpu.VMEM((4, 8, LEN), f32),
            pltpu.VMEM((8, LEN), f32),
            pltpu.VMEM((3, 8, 8, LEN), f32),
            dma((8,)), dma(()),
            dma((8,)), dma((8,)),
            dma((2,)), dma((2,)),
            dma((2, 2, 8)), dma((2, 2, 8)),
            dma((2, 2, 2, 4)), dma((2, 2, 2, 4)),
            dma((2, 2, 2, 4)), dma((2, 2, 2, 4)),
            dma((2, 2, 8)), dma((2, 2, 8)),
            dma((2,)), dma((2,)),
            dma((8,)), dma((8,)),
            dma(()), dma(()),
            dma((3, 8)), dma((3, 8)),
            dma(()), dma(()),
            dma((3, 8)), dma((3, 8)),
        ],
        compiler_params=pltpu.CompilerParams(
            collective_id=0, has_side_effects=True, vmem_limit_bytes=VMEM_LIMIT
        ),
        name="exchange",
    )(
        tile_rows.reshape(SLOTS), tile_cols.reshape(SLOTS), counts, basis, previous, coupling,
        energies.reshape(1, LEN), tile_values.reshape(SLOTS, LEN, LEN),
    )
    return pl.pallas_call(
        deliver_kernel,
        out_shape=(
            jax.ShapeDtypeStruct((K, K), f32),
            jax.ShapeDtypeStruct((K, K), f32),
            jax.ShapeDtypeStruct((K, LEN), f32),
        ),
        in_specs=[vmem],
        out_specs=(vmem, vmem, vmem),
        compiler_params=pltpu.CompilerParams(vmem_limit_bytes=VMEM_LIMIT),
        name="deliver",
    )(out)


def solution(mesh):
    split_mesh = Mesh(mesh.devices.reshape(4, 2, 8, 8, 2), AXES)
    both = ROW + COL
    in_specs = (
        P(None, both),
        P(None, both),
        P(),
        P(both),
        P(ROW, COL, None, None, None),
        P(ROW, COL, None),
        P(ROW, COL, None),
        P(ROW, COL),
    )
    out_specs = (P(), P(), P(None, both))
    return jax.shard_map(
        shards, mesh=split_mesh, in_specs=in_specs, out_specs=out_specs, check_vma=False
    )
```
